32 devices in a mesh: owner: 16 (over z, y, x), replica: 2 (over core).
Axes of the slice: x: 2, y: 2, z: 4, core: 2. Of those that a mesh axis runs over, the one named last changes fastest.
Arguments:
- queries: bfloat16 [256, 32, 128], P(('owner', 'replica')), may hold values from -8 to 8
- pages: bfloat16 [16, 1024, 128], P('owner'), may hold values from -3 to 3
- pair_page: int32 [2048, 1], P(('owner', 'replica')), may hold values from 0 to 15, as said below
- pair_query: int32 [2048], P(('owner', 'replica')), may hold values from 0 to 7
- pair_label: int32 [2048], P(('owner', 'replica')), may hold values 0 or 1
- hot_pages: int32 [2], replicated, may hold values from 0 to 15, as said below
Outputs:
- query_grad: bfloat16 [256, 32, 128], P(('owner', 'replica'))
- page_grad: bfloat16 [16, 1024, 128], P('owner', 'replica')
The draws below stay inside these ranges and needn't reach their ends.
Inputs may be any that keep to these rules, and one draw needn't show every extreme that they name: `pair_page`: the rows of one device name no page more than 16 times, and some page exactly 16 times. `hot_pages`: 2 different page numbers; the last page is always among them.
All inputs are finite; a program needn't handle non-finite values. No bound on the sum of `pair_label` on one device may be relied on, other than what follows from the above.
Results may differ from the reference program's by a relative error of at most 0.0085.
Values may be sent and summed in bfloat16 or wider, within the bound.
A program may use at most 64 MiB of HBM per device.

```python
import math
import jax
import jax.numpy as jnp
from jax import lax

W = 128
QT = 32
PATCHES = 1024
HOT = 2
Q_DEV = 8
PAIR_DEV = 64
CAP = 16
PAGES = 16
QUERIES = 256
PAIRS = 2048


def shared_draw(key):
    page_key = jax.random.fold_in(key, 11)
    query_key = jax.random.fold_in(key, 12)
    spread = W ** (-0.25)
    page_vals = spread * jax.random.normal(page_key, (PAGES, PATCHES, W), jnp.float32)
    query_vals = spread * jax.random.normal(query_key, (QUERIES, QT, W), jnp.float32)
    return (jnp.clip(page_vals, -3.0, 3.0), jnp.clip(query_vals, -8.0, 8.0))


def draw_pages(key, part):
    return shared_draw(key)[0].astype(jnp.bfloat16)


def draw_queries(key, part):
    return shared_draw(key)[1].astype(jnp.bfloat16)


def hot_list(key):
    others = jax.random.permutation(jax.random.fold_in(key, 21), PAGES - 1)[:HOT - 1].astype(jnp.int32)
    last_page = jnp.full((1,), PAGES - 1, jnp.int32)
    return jnp.concatenate([last_page, others]).astype(jnp.int32)


def page_lists(key):
    flagged = hot_list(key)
    numbers = jnp.arange(PAGES, dtype=jnp.int32)
    is_flagged = jnp.any(numbers[:, None] == flagged[None, :], axis=1).astype(jnp.int32)

    def one_device(device):
        device_key = jax.random.fold_in(jax.random.fold_in(key, 22), device)
        shuffled = jax.random.permutation(jax.random.fold_in(device_key, 1), PAGES).astype(jnp.int32)
        ranking = is_flagged[shuffled] * PAGES + numbers
        cold_first = shuffled[jnp.argsort(ranking, stable=True)]
        others = jnp.tile(cold_first[:PAGES - HOT], CAP)[:PAIR_DEV - HOT * CAP]
        listed = jnp.concatenate([jnp.repeat(flagged, CAP), others]).astype(jnp.int32)
        mixing = jax.random.permutation(jax.random.fold_in(device_key, 2), PAIR_DEV)
        return listed[mixing]
    rows = jax.vmap(one_device)(jnp.arange(PAIRS // PAIR_DEV, dtype=jnp.int32))
    return rows.reshape(PAIRS, 1).astype(jnp.int32)


def draw_pair_page(key, part):
    return page_lists(key)


def draw_hot_pages(key, part):
    return hot_list(key)


def with_ends(drawn, rng, least, high):
    dims = drawn.shape
    index_at = [jax.random.randint(jax.random.fold_in(rng, axis), (), 0, dims[axis]) for axis in range(len(dims))]
    drawn = drawn.at[tuple(index_at)].set(least)
    longest = dims.index(max(dims))
    index_at[longest] = (index_at[longest] + 1) % dims[longest]
    return drawn.at[tuple(index_at)].set(high)


def setup_inputs(seed: int = 0) -> dict:
    keys = jax.random.split(jax.random.key(seed), 7)
    queries = draw_queries(jax.random.fold_in(keys[6], 71), 0)
    pages = draw_pages(jax.random.fold_in(keys[6], 71), 0)
    pair_page = draw_pair_page(jax.random.fold_in(keys[6], 71), 0)
    pair_query = with_ends(jax.random.randint(keys[3], (PAIRS,), 0, Q_DEV), jax.random.fold_in(keys[3], 1), 0, Q_DEV - 1).astype(jnp.int32)
    pair_label = with_ends((jax.random.randint(keys[4], (PAIRS,), 0, 4) < 1).astype(jnp.int32), jax.random.fold_in(keys[4], 1), 0, 1)
    hot_pages = draw_hot_pages(jax.random.fold_in(keys[6], 71), 0)
    return {"queries": queries, "pages": pages, "pair_page": pair_page, "pair_query": pair_query, "pair_label": pair_label, "hot_pages": hot_pages}


SHARPNESS = 4.0
SLOPE_SCALE = 0.5
HOT_SHIFT = 2.0


def reference(queries, pages, pair_page, pair_query, pair_label, hot_pages):
    owner_ids = pair_page[:, 0].astype(jnp.int32)
    query_ids = ((jnp.arange(PAIRS, dtype=jnp.int32) // PAIR_DEV) * Q_DEV + pair_query).astype(jnp.int32)
    labels = pair_label.astype(jnp.float32)
    hot_flag = jnp.any(owner_ids[:, None] == hot_pages[None, :].astype(jnp.int32), axis=1).astype(jnp.float32)
    offset = -SLOPE_SCALE * QT * (math.log(PATCHES) / SHARPNESS + SHARPNESS / 2.0)
    group_size = 64
    groups = PAIRS // group_size

    def step(carry, inputs):
        owner_part, query_part, label_part, hot_part = inputs
        query_rows = queries[query_part].astype(jnp.float32)
        page_rows = pages[owner_part].astype(jnp.float32)
        logits = SHARPNESS * jnp.einsum("btw,bpw->btp", query_rows, page_rows)
        peak = jnp.max(logits, axis=2, keepdims=True)
        expo = jnp.exp(logits - peak)
        totals = jnp.sum(expo, axis=2, keepdims=True)
        log_total = peak + jnp.log(totals)
        score = jnp.sum(log_total[:, :, 0], axis=1) / SHARPNESS
        logit = SLOPE_SCALE * score + offset - HOT_SHIFT * hot_part
        slope = SLOPE_SCALE * (jax.nn.sigmoid(logit) - label_part)
        weight = (expo / totals * slope[:, None, None]).astype(jnp.bfloat16)
        weight_wide = weight.astype(jnp.float32)
        grads = jnp.einsum("btp,bpw->btw", weight_wide, page_rows).astype(jnp.bfloat16)
        page_part = jnp.einsum("btp,btw->bpw", weight_wide, query_rows)
        carry = carry.at[owner_part].add(page_part)
        return carry, grads

    start = jnp.zeros((PAGES, PATCHES, W), jnp.float32)
    final, parts = lax.scan(step, start, (owner_ids.reshape(groups, group_size), query_ids.reshape(groups, group_size), labels.reshape(groups, group_size), hot_flag.reshape(groups, group_size)))
    query_grad = jax.ops.segment_sum(parts.reshape(PAIRS, QT, W).astype(jnp.float32), query_ids, num_segments=QUERIES)
    return query_grad.astype(jnp.bfloat16), final.astype(jnp.bfloat16)
```

```python
import functools
import math

import jax
import jax.numpy as jnp
from jax import lax
from jax.experimental import pallas as pl
from jax.experimental.pallas import tpu as pltpu
from jax.sharding import PartitionSpec as P

MESH = pl.DeviceIdType.MESH


ORDER = range(4)

def plan():
    return (
        ("tokens", 1),
        ("block", (1, 0)),
        ("page", 1),
        ("page", 2),
        ("page", 3),
        ("tokens", 3),
        ("tokens", 2),
        ("block", (3, 0), (2, 0)),
        ("finish", 0),
        ("relayed", 3),
        ("block", (0, 3), (1, 3), (3, 3), (2, 3)),
        ("finish", 3),
        ("relayed", 1),
        ("block", (0, 1), (1, 1), (3, 1), (2, 1)),
        ("finish", 1),
        ("share", 3),
        ("relayed", 2),
        ("block", (2, 2), (3, 2)),
        ("line", 2),
        ("line", 3),
        ("share", 1),
        ("block", (1, 2), (0, 2)),
        ("line", 1),
        ("finish", 2),
        ("share", 2),
    )


def dense_kernel(
    lines,
    planes,
    shapes,
    query_ref,
    page_ref,
    pair_page_hbm,
    pair_query_hbm,
    pair_label_hbm,
    hot_hbm,
    query_grad_ref,
    page_grad_ref,
    pair_page_ref,
    pair_query_ref,
    pair_label_ref,
    hot_ref,
    held,
    paged,
    page_acc,
    query_acc,
    page_rows,
    swap_out,
    swap_in,
    share_out,
    share_in,
    part_out,
    part_in,
    load_sem,
    line_sem,
    line_in_sem,
    flag_sem,
    flag_in_sem,
    plane_sem,
    plane_in_sem,
    relay_sem,
    relay_in_sem,
    swap_sem,
    swap_in_sem,
    share_sem,
    share_in_sem,
    part_sem,
    part_in_sem,
):
    local_queries, tokens_each, width, patches = shapes
    rows = local_queries * tokens_each
    flag_rows = held.shape[1] - rows
    me = lax.axis_index("owner")
    core = lax.axis_index("replica")
    my_line, my_plane = me // planes, me % planes

    def load(src, dst, place):
        return pltpu.make_async_copy(src, dst, load_sem.at[place])

    loads = [
        load(pair_page_hbm, pair_page_ref, 0),
        load(pair_query_hbm, pair_query_ref, 1),
        load(pair_label_hbm, pair_label_ref, 2),
        load(hot_hbm, hot_ref, 3),
        load(query_ref, held.at[my_line, pl.ds(0, rows), :], 4),
        load(page_ref, paged.at[my_plane], 5),
    ]

    barrier = pltpu.get_barrier_semaphore()

    def greet(owner):
        pl.semaphore_signal(barrier, inc=1, device_id={"owner": owner}, device_id_type=MESH)

    for step in range(1, lines):
        greet((my_line ^ step) * planes + my_plane)
    for step in range(1, planes):
        greet(my_line * planes + (my_plane ^ step))
    pl.semaphore_signal(barrier, inc=1, device_id={"replica": 1 - core}, device_id_type=MESH)
    for copy in loads:
        copy.start()

    def remote(src, dst, sent, received, device):
        return pltpu.make_async_remote_copy(
            src_ref=src,
            dst_ref=dst,
            send_sem=sent,
            recv_sem=received,
            device_id=device,
            device_id_type=MESH,
        )

    def to_line(line):
        return {"owner": line * planes + my_plane}

    def to_plane(plane):
        return {"owner": my_line * planes + plane}

    twin = {"replica": 1 - core}

    def tokens_to(line):
        dst = held.at[my_line, pl.ds(0, rows), :]
        return remote(query_ref, dst, line_sem.at[line], line_in_sem.at[my_line], to_line(line))

    def tokens_from(line):
        slot = held.at[line, pl.ds(0, rows), :]
        return remote(slot, slot, line_sem.at[line], line_in_sem.at[line], to_line(line))

    def flags_to(line):
        slot = held.at[my_line, pl.ds(rows, flag_rows), :]
        return remote(slot, slot, flag_sem.at[line], flag_in_sem.at[my_line], to_line(line))

    def flags_from(line):
        slot = held.at[line, pl.ds(rows, flag_rows), :]
        return remote(slot, slot, flag_sem.at[line], flag_in_sem.at[line], to_line(line))

    def page_to(plane):
        src, dst = page_ref.at[core], paged.at[my_plane, core]
        return remote(src, dst, plane_sem.at[plane], plane_in_sem.at[my_plane], to_plane(plane))

    def page_from(plane):
        slot = paged.at[plane, core]
        return remote(slot, slot, plane_sem.at[plane], plane_in_sem.at[plane], to_plane(plane))

    def relay(plane):
        slot = paged.at[plane, core]
        return remote(slot, slot, relay_sem.at[plane], relay_in_sem.at[plane], twin)

    def relayed(plane):
        slot = paged.at[plane, 1 - core]
        return remote(slot, slot, relay_sem.at[plane], relay_in_sem.at[plane], twin)

    def swap(plane):
        return remote(
            swap_out.at[plane], swap_in.at[plane], swap_sem.at[plane], swap_in_sem.at[plane], twin
        )

    def share_to(plane):
        dst = share_in.at[my_plane]
        sent, received = share_sem.at[plane], share_in_sem.at[my_plane]
        return remote(share_out.at[plane], dst, sent, received, to_plane(plane))

    def share_from(plane):
        dst = share_in.at[plane]
        sent, received = share_sem.at[plane], share_in_sem.at[plane]
        return remote(share_out.at[plane], dst, sent, received, to_plane(plane))

    def part_to(line):
        dst = part_in.at[my_line]
        sent, received = part_sem.at[line], part_in_sem.at[my_line]
        return remote(part_out.at[line], dst, sent, received, to_line(line))

    def part_from(line):
        dst = part_in.at[line]
        sent, received = part_sem.at[line], part_in_sem.at[line]
        return remote(part_out.at[line], dst, sent, received, to_line(line))

    pl.semaphore_wait(barrier, lines + planes - 1)
    page_to(my_plane ^ 1).start()
    page_to(my_plane ^ 2).start()
    tokens_to(my_line ^ 1).start()
    tokens_to(my_line ^ 3).start()
    tokens_to(my_line ^ 2).start()
    page_to(my_plane ^ 3).start()

    pairs = pair_page_ref.shape[1]
    lanes = held.shape[2]
    for copy in loads[:4]:
        copy.wait()
    page_hot = (
        lax.broadcasted_iota(jnp.int32, (lanes, pairs), 0) == pair_page_ref[...]
    ).astype(jnp.float32)
    query_hot = lax.broadcasted_iota(jnp.int32, (local_queries, pairs), 0) == pair_query_ref[...]
    counted = query_hot.astype(jnp.float32)
    labelled = counted * pair_label_ref[...].astype(jnp.float32)
    stacked = jnp.concatenate([counted, labelled], axis=0)
    flags = lax.dot_general(
        stacked, page_hot, (((1,), (1,)), ((), ())), preferred_element_type=jnp.float32
    )
    held[my_line, pl.ds(rows, flag_rows), :] = flags.astype(jnp.bfloat16)
    for step in range(1, lines):
        flags_to(my_line ^ step).start()

    offset = -0.5 * tokens_each * (math.log(patches) / 4.0 + 2.0)

    row_query = lax.broadcasted_iota(jnp.int32, (rows, flag_rows), 0) // tokens_each
    flag_row = lax.broadcasted_iota(jnp.int32, (rows, flag_rows), 1)
    count_pick = (flag_row == row_query).astype(jnp.bfloat16)
    label_pick = (flag_row == row_query + local_queries).astype(jnp.bfloat16)
    lane = lax.broadcasted_iota(jnp.int32, (1, lanes), 1)
    scale = 4.0 * math.log2(math.e)

    def logits(line, plane):
        return lax.dot_general(
            held[line, pl.ds(0, rows), :],
            paged[plane].reshape(patches, width),
            (((1,), (1,)), ((), ())),
            preferred_element_type=jnp.float32,
        )

    def weights(dots, line, plane):
        page = my_line * planes + plane
        own_lane = (lane == page).astype(jnp.float32)
        own_shift = 2.0 * jnp.sum((hot_ref[...] == page).astype(jnp.float32), keepdims=True)
        flag = held[line, pl.ds(rows, flag_rows), :]
        counts = jnp.sum(
            jnp.dot(count_pick, flag, preferred_element_type=jnp.float32) * own_lane,
            axis=1,
            keepdims=True,
        )
        labels = jnp.sum(
            jnp.dot(label_pick, flag, preferred_element_type=jnp.float32) * own_lane,
            axis=1,
            keepdims=True,
        )
        peak = jnp.max(dots, axis=1, keepdims=True)
        expo = jnp.exp2((dots - peak) * scale)
        totals = jnp.sum(expo, axis=1, keepdims=True)
        log_total = 4.0 * peak + jnp.log(totals)
        score = jnp.sum(log_total.reshape(local_queries, tokens_each, 1), axis=1, keepdims=True)
        score = jnp.broadcast_to(score, (local_queries, tokens_each, 1)).reshape(rows, 1)
        logit = 0.5 * (score / 4.0) + offset - own_shift
        slope = 0.5 * (counts * jax.nn.sigmoid(logit) - labels)
        return (expo * (slope / totals)).astype(jnp.bfloat16)

    started_lines, started_pages = set(), set()

    def gradients(weight, line, plane, first_line, first_page):
        tokens = held[line, pl.ds(0, rows), :]
        by_query = jnp.dot(
            weight, paged[plane].reshape(patches, width), preferred_element_type=jnp.float32
        )
        by_page = lax.dot_general(
            tokens, weight, (((0,), (0,)), ((), ())), preferred_element_type=jnp.float32
        )
        query_acc[line] = by_query if first_line else query_acc[line] + by_query
        page_acc[plane] = by_page if first_page else page_acc[plane] + by_page

    def block(*places):
        spots = [(my_line ^ hop, my_plane ^ jump) for hop, jump in places]
        dots = [logits(*spot) for spot in spots]
        for spot, dot, (hop, jump) in zip(spots, dots, places):
            fresh = hop not in started_lines, jump not in started_pages
            started_lines.add(hop)
            started_pages.add(jump)
            gradients(weights(dot, *spot), *spot, *fresh)

    def half_page(plane):
        swap(plane).wait_recv()
        return page_rows[plane, core] + swap_in[plane].astype(jnp.float32)

    def act(kind, *what):
        if kind == "block":
            block(*what)
            return
        offset_by = what[0]
        line, plane = my_line ^ offset_by, my_plane ^ offset_by
        if kind == "tokens":
            tokens_from(line).wait_recv()
            flags_from(line).wait_recv()
        elif kind == "send_tokens":
            tokens_to(line).start()
        elif kind == "sent_tokens":
            tokens_to(line).wait_send()
        elif kind == "send_page":
            page_to(plane).start()
        elif kind == "sent_page":
            page_to(plane).wait_send()
        elif kind == "page":
            page_from(plane).wait_recv()
            relay(plane).start()
        elif kind == "relayed":
            relayed(plane).wait_recv()
        elif kind == "line":
            part_out[line] = query_acc[line].astype(jnp.bfloat16)
            part_to(line).start()
        elif kind == "finish":
            page_rows[plane] = page_acc[plane].T.reshape(page_rows.shape[1:])
            swap_out[plane] = page_rows[plane, 1 - core].astype(jnp.bfloat16)
            swap(plane).start()
        elif kind == "share":
            share_out[plane] = half_page(plane).astype(jnp.bfloat16)
            share_to(plane).start()

    loads[4].wait()
    loads[5].wait()
    block((0, 0))
    for step in plan():
        act(*step)

    total = half_page(my_plane)
    for step in range(1, planes):
        share_from(my_plane ^ step).wait_recv()
        total += share_in[my_plane ^ step].astype(jnp.float32)
    page_grad_ref[...] = total.astype(jnp.bfloat16)

    total = query_acc[my_line]
    for step in range(1, lines):
        part_from(my_line ^ step).wait_recv()
        total += part_in[my_line ^ step].astype(jnp.float32)
    query_grad_ref[...] = total.astype(jnp.bfloat16)

    swap(my_plane).wait_send()
    for step in range(1, lines):
        flags_to(my_line ^ step).wait_send()
        part_to(my_line ^ step).wait_send()
    for step in range(1, planes):
        plane = my_plane ^ step
        relay(plane).wait_send()
        swap(plane).wait_send()
        share_to(plane).wait_send()
    tokens_to(my_line ^ 1).wait_send()
    tokens_to(my_line ^ 2).wait_send()
    tokens_to(my_line ^ 3).wait_send()
    page_to(my_plane ^ 1).wait_send()
    page_to(my_plane ^ 2).wait_send()
    page_to(my_plane ^ 3).wait_send()


def dense_shards(queries, pages, pair_page, pair_query, pair_label, hot_pages):
    owners = lax.axis_size("owner")
    replicas = lax.axis_size("replica")
    local_queries, tokens_each, width = queries.shape
    patches = pages.shape[1]
    pairs = pair_query.shape[0]
    rows = local_queries * tokens_each
    flag_rows = 2 * local_queries
    part = patches // replicas
    planes = math.isqrt(owners)
    lines = owners // planes
    vmem = pl.BlockSpec(memory_space=pltpu.VMEM)
    hbm = pl.BlockSpec(memory_space=pltpu.HBM)
    query_grad, page_grad = pl.pallas_call(
        functools.partial(
            dense_kernel, lines, planes, (local_queries, tokens_each, width, patches)
        ),
        out_shape=(
            jax.ShapeDtypeStruct((rows, width), jnp.bfloat16),
            jax.ShapeDtypeStruct((part, width), jnp.bfloat16),
        ),
        in_specs=[hbm] * 6,
        out_specs=(vmem, vmem),
        scratch_shapes=[
            *[pltpu.VMEM((1, pairs), jnp.int32)] * 3,
            pltpu.VMEM((1, hot_pages.shape[0]), jnp.int32),
            pltpu.VMEM((lines, rows + flag_rows, width), jnp.bfloat16),
            pltpu.VMEM((planes, replicas, part, width), jnp.bfloat16),
            pltpu.VMEM((planes, width, patches), jnp.float32),
            pltpu.VMEM((lines, rows, width), jnp.float32),
            pltpu.VMEM((planes, replicas, part, width), jnp.float32),
            *[pltpu.VMEM((planes, part, width), jnp.bfloat16)] * 4,
            *[pltpu.VMEM((lines, rows, width), jnp.bfloat16)] * 2,
            pltpu.SemaphoreType.DMA((6,)),
            *[pltpu.SemaphoreType.DMA((lines,))] * 4,
            *[pltpu.SemaphoreType.DMA((planes,))] * 8,
            *[pltpu.SemaphoreType.DMA((lines,))] * 2,
        ],
        compiler_params=pltpu.CompilerParams(
            collective_id=0, has_side_effects=True, vmem_limit_bytes=24 << 20
        ),
    )(
        *[
            pltpu.with_memory_space_constraint(operand, pltpu.HBM)
            for operand in (
                queries.reshape(rows, width),
                pages[0].reshape(replicas, part, width),
                pair_page.reshape(1, pairs),
                pair_query.reshape(1, pairs),
                pair_label.reshape(1, pairs),
                hot_pages.reshape(1, hot_pages.shape[0]),
            )
        ]
    )
    return query_grad.reshape(queries.shape), page_grad[None]


SHARPNESS = 4.0
SLOPE_SCALE = 0.5
HOT_SHIFT = 2.0


def score_block(token_rows, label_rows, page_rows, offset, shift):
    count = token_rows.shape[0]
    tokens_each = token_rows.shape[1]
    flat_rows = token_rows.reshape(count * tokens_each, token_rows.shape[2])
    logits = SHARPNESS * lax.dot_general(
        flat_rows, page_rows, (((1,), (1,)), ((), ())), preferred_element_type=jnp.float32
    )
    peak = jnp.max(logits, axis=1, keepdims=True)
    expo = jnp.exp(logits - peak)
    totals = jnp.sum(expo, axis=1, keepdims=True)
    log_total = peak + jnp.log(totals)
    score = jnp.sum(log_total.reshape(count, tokens_each), axis=1) / SHARPNESS
    logit = SLOPE_SCALE * score + offset - shift
    slope = SLOPE_SCALE * (jax.nn.sigmoid(logit) - label_rows[:, 0]) * label_rows[:, 1]
    slope_rows = jnp.repeat(slope, tokens_each)[:, None]
    weight = (expo / totals * slope_rows).astype(jnp.bfloat16)
    grads = jnp.dot(weight, page_rows, preferred_element_type=jnp.float32).astype(jnp.bfloat16)
    page_part = lax.dot_general(
        weight, flat_rows, (((0,), (0,)), ((), ())), preferred_element_type=jnp.float32
    )
    return (grads.reshape(token_rows.shape), page_part)


def sparse_shards(queries, pages, pair_page, pair_query, pair_label, hot_pages):
    owners = lax.axis_size("owner")
    owner_place = lax.axis_index("owner")
    local_pairs = pair_page.shape[0]
    local_queries = queries.shape[0]
    tokens_each = queries.shape[1]
    width = queries.shape[2]
    patch_count = pages.shape[1]
    capacity = max(2, 4 * local_pairs // owners)
    slots = owners * capacity
    offset = -SLOPE_SCALE * tokens_each * (math.log(patch_count) / SHARPNESS + SHARPNESS / 2.0)
    targets = pair_page[:, 0]
    owned_hot = (hot_pages == owner_place).astype(jnp.float32)
    target_hot = (targets[:, None] == jnp.arange(owners, dtype=jnp.int32)[None, :]).astype(
        jnp.int32
    )
    earlier = jnp.cumsum(target_hot, axis=0) - target_hot
    rank_within = jnp.sum(earlier * target_hot, axis=1)
    slot_of = targets * capacity + rank_within
    select = (slot_of[None, :] == jnp.arange(slots, dtype=jnp.int32)[:, None]).astype(jnp.bfloat16)
    query_hot = (pair_query[:, None] == jnp.arange(local_queries, dtype=jnp.int32)[None, :]).astype(
        jnp.bfloat16
    )
    pair_tokens = jnp.dot(
        query_hot,
        queries.reshape(local_queries, tokens_each * width),
        preferred_element_type=jnp.float32,
    ).astype(jnp.bfloat16)
    send_tokens = jnp.dot(select, pair_tokens, preferred_element_type=jnp.float32).astype(
        jnp.bfloat16
    )
    pair_flags = jnp.stack(
        [pair_label.astype(jnp.float32), jnp.ones((local_pairs,), jnp.float32)], axis=1
    ).astype(jnp.bfloat16)
    send_flags = jnp.dot(select, pair_flags, preferred_element_type=jnp.float32).astype(
        jnp.bfloat16
    )
    got_tokens, got_flags = (
        lax.all_to_all(
            send_tokens.reshape(owners, capacity * tokens_each * width),
            "owner",
            split_axis=0,
            concat_axis=0,
            tiled=True,
        ),
        lax.all_to_all(
            send_flags.reshape(owners, capacity * 2),
            "owner",
            split_axis=0,
            concat_axis=0,
            tiled=True,
        ),
    )
    slot_tokens = got_tokens.reshape(slots, tokens_each, width)
    slot_flags = got_flags.reshape(slots, 2).astype(jnp.float32)
    page_rows = pages[0]
    own_shift = HOT_SHIFT * jnp.sum(owned_hot)
    block_rows = slots // max(1, slots // 64)
    filled = (slot_flags[:, 1] > 0.5).astype(jnp.int32)
    order = jnp.argsort(1 - filled, stable=True)
    inverse = jnp.argsort(order, stable=True)
    sorted_tokens = slot_tokens[order]
    sorted_flags = slot_flags[order]
    live_blocks = (jnp.sum(filled) + block_rows - 1) // block_rows

    def visit(block_id, carry):
        grad_store, page_acc = carry
        start = (block_id * block_rows).astype(jnp.int32)
        token_rows = lax.dynamic_slice_in_dim(sorted_tokens, start, block_rows, 0)
        label_rows = lax.dynamic_slice_in_dim(sorted_flags, start, block_rows, 0)
        grads, page_part = score_block(token_rows, label_rows, page_rows, offset, own_shift)
        grad_store = lax.dynamic_update_slice_in_dim(grad_store, grads, start, 0)
        return (grad_store, page_acc + page_part)

    sorted_grads, page_terms = lax.fori_loop(
        0,
        live_blocks,
        visit,
        (
            jnp.zeros((slots, tokens_each, width), jnp.bfloat16),
            jnp.zeros((patch_count, width), jnp.float32),
        ),
    )
    slot_grads = sorted_grads[inverse]
    returned = lax.all_to_all(
        slot_grads.reshape(owners, capacity * tokens_each * width),
        "owner",
        split_axis=0,
        concat_axis=0,
        tiled=True,
    )
    pair_grads = lax.dot_general(
        select,
        returned.reshape(slots, tokens_each * width),
        (((0,), (0,)), ((), ())),
        preferred_element_type=jnp.float32,
    )
    summed = lax.dot_general(
        query_hot.astype(jnp.float32),
        pair_grads,
        (((0,), (0,)), ((), ())),
        precision=lax.Precision.HIGHEST,
        preferred_element_type=jnp.float32,
    )
    query_grad = summed.reshape(local_queries, tokens_each, width).astype(jnp.bfloat16)
    page_share = lax.psum_scatter(
        page_terms.astype(jnp.bfloat16), "replica", scatter_dimension=0, tiled=True
    )
    return (query_grad, page_share[None])


def shards(queries, pages, pair_page, pair_query, pair_label, hot_pages):
    owners = lax.axis_size("owner")
    replicas = lax.axis_size("replica")
    local_pairs = pair_query.shape[0]
    local_queries = queries.shape[0]
    capacity = max(2, 4 * local_pairs // owners)
    dense = capacity >= local_queries and owners <= queries.shape[2] and replicas == 2
    dense = dense and owners == len(ORDER) ** 2
    plan = dense_shards if dense else sparse_shards
    return plan(queries, pages, pair_page, pair_query, pair_label, hot_pages)


def solution(mesh):
    placed = (
        P(("owner", "replica"), None, None),
        P("owner", None, None),
        P(("owner", "replica"), None),
        P(("owner", "replica")),
        P(("owner", "replica")),
        P(),
    )
    return jax.shard_map(
        shards,
        mesh=mesh,
        in_specs=placed,
        out_specs=(P(("owner", "replica"), None, None), P("owner", "replica", None)),
        check_vma=False,
    )
```

```python
import functools
import math

import jax
import jax.numpy as jnp
from jax import lax
from jax.experimental import pallas as pl
from jax.experimental.pallas import tpu as pltpu
from jax.sharding import PartitionSpec as P

MESH = pl.DeviceIdType.MESH


ORDER = range(4)

def plan():
    return (
        ("tokens", 1),
        ("block", (1, 0)),
        ("page", 1),
        ("send_page", 3),
        ("send_tokens", 2),
        ("block", (0, 1), (1, 1)),
        ("tokens", 3),
        ("block", (3, 1), (3, 0)),
        ("relayed", 2),
        ("block", (0, 2), (1, 2), (3, 2)),
        ("page", 3),
        ("tokens", 2),
        ("block", (2, 1), (2, 2)),
        ("finish", 1),
        ("finish", 2),
        ("relayed", 3),
        ("block", (3, 3), (2, 3)),
        ("line", 3),
        ("share", 1),
        ("share", 2),
        ("block", (2, 0), (1, 3), (0, 3)),
        ("finish", 3),
        ("line", 2),
        ("line", 1),
        ("finish", 0),
        ("share", 3),
    )


def dense_kernel(
    lines,
    planes,
    shapes,
    query_ref,
    page_ref,
    pair_page_hbm,
    pair_query_hbm,
    pair_label_hbm,
    hot_hbm,
    query_grad_ref,
    page_grad_ref,
    pair_page_ref,
    pair_query_ref,
    pair_label_ref,
    hot_ref,
    held,
    paged,
    page_acc,
    query_acc,
    swap_out,
    swap_in,
    share_out,
    share_in,
    part_out,
    part_in,
    load_sem,
    line_sem,
    line_in_sem,
    flag_sem,
    flag_in_sem,
    plane_sem,
    plane_in_sem,
    relay_sem,
    relay_in_sem,
    swap_sem,
    swap_in_sem,
    share_sem,
    share_in_sem,
    part_sem,
    part_in_sem,
):
    local_queries, tokens_each, width, patches = shapes
    rows = local_queries * tokens_each
    flag_rows = held.shape[1] - rows
    part = page_acc.shape[3]
    me = lax.axis_index("owner")
    core = lax.axis_index("replica")
    my_line, my_plane = me // planes, me % planes

    def load(src, dst, place):
        return pltpu.make_async_copy(src, dst, load_sem.at[place])

    loads = [
        load(pair_page_hbm, pair_page_ref, 0),
        load(pair_query_hbm, pair_query_ref, 1),
        load(pair_label_hbm, pair_label_ref, 2),
        load(hot_hbm, hot_ref, 3),
        load(query_ref, held.at[my_line, pl.ds(0, rows), :], 4),
        load(page_ref, paged.at[my_plane], 5),
    ]

    barrier = pltpu.get_barrier_semaphore()

    def greet(owner):
        pl.semaphore_signal(barrier, inc=1, device_id={"owner": owner}, device_id_type=MESH)

    for step in range(1, lines):
        greet((my_line ^ step) * planes + my_plane)
    for step in range(1, planes):
        greet(my_line * planes + (my_plane ^ step))
    pl.semaphore_signal(barrier, inc=1, device_id={"replica": 1 - core}, device_id_type=MESH)
    across = {"owner": my_line * planes + (my_plane ^ (1 + core)), "replica": 1 - core}
    pl.semaphore_signal(barrier, inc=1, device_id=across, device_id_type=MESH)
    for copy in loads:
        copy.start()

    def remote(src, dst, sent, received, device):
        return pltpu.make_async_remote_copy(
            src_ref=src,
            dst_ref=dst,
            send_sem=sent,
            recv_sem=received,
            device_id=device,
            device_id_type=MESH,
        )

    def to_line(line):
        return {"owner": line * planes + my_plane}

    def to_plane(plane):
        return {"owner": my_line * planes + plane}

    twin = {"replica": 1 - core}

    def tokens_to(line):
        slot = held.at[my_line, pl.ds(0, rows), :]
        return remote(slot, slot, line_sem.at[line], line_in_sem.at[my_line], to_line(line))

    def tokens_from(line):
        slot = held.at[line, pl.ds(0, rows), :]
        return remote(slot, slot, line_sem.at[line], line_in_sem.at[line], to_line(line))

    def flags_to(line):
        slot = held.at[my_line, pl.ds(rows, flag_rows), :]
        return remote(slot, slot, flag_sem.at[line], flag_in_sem.at[my_line], to_line(line))

    def flags_from(line):
        slot = held.at[line, pl.ds(rows, flag_rows), :]
        return remote(slot, slot, flag_sem.at[line], flag_in_sem.at[line], to_line(line))

    def turn(jump):
        return my_plane ^ (0, 1 + core, 2 - core, 3)[jump]

    def page_to(jump):
        slot = paged.at[my_plane, core]
        plane = my_plane ^ jump
        device = {"owner": my_line * planes + plane, "replica": jump - 1}
        return remote(slot, slot, plane_sem.at[plane], plane_in_sem.at[my_plane, core], device)

    def page_on():
        slot = paged.at[turn(1), core]
        sent, received = plane_sem.at[turn(3)], plane_in_sem.at[turn(1), core]
        return remote(slot, slot, sent, received, to_plane(turn(2)))

    def page_from(plane, side):
        slot = paged.at[plane, side]
        sent, received = plane_sem.at[plane], plane_in_sem.at[plane, side]
        return remote(slot, slot, sent, received, to_plane(plane))

    def relay(jump):
        plane = turn(jump)
        slot = paged.at[plane] if jump < 3 else paged.at[plane, core]
        return remote(slot, slot, relay_sem.at[plane], relay_in_sem.at[plane], twin)

    def relayed(jump):
        plane = turn(jump)
        slot = paged.at[plane] if jump < 3 else paged.at[plane, 1 - core]
        return remote(slot, slot, relay_sem.at[plane], relay_in_sem.at[plane], twin)

    def swap(plane):
        return remote(
            swap_out.at[plane], swap_in.at[plane], swap_sem.at[plane], swap_in_sem.at[plane], twin
        )

    def share_to(plane):
        dst = share_in.at[my_plane]
        sent, received = share_sem.at[plane], share_in_sem.at[my_plane]
        return remote(share_out.at[plane], dst, sent, received, to_plane(plane))

    def share_from(plane):
        dst = share_in.at[plane]
        sent, received = share_sem.at[plane], share_in_sem.at[plane]
        return remote(share_out.at[plane], dst, sent, received, to_plane(plane))

    def part_to(line):
        dst = part_in.at[my_line]
        sent, received = part_sem.at[line], part_in_sem.at[my_line]
        return remote(part_out.at[line], dst, sent, received, to_line(line))

    def part_from(line):
        dst = part_in.at[line]
        sent, received = part_sem.at[line], part_in_sem.at[line]
        return remote(part_out.at[line], dst, sent, received, to_line(line))

    loads[4].wait()
    loads[5].wait()
    pl.semaphore_wait(barrier, lines + planes)
    page_to(1).start()
    page_to(2).start()
    tokens_to(my_line ^ 1).start()
    tokens_to(my_line ^ 3).start()

    pairs = pair_page_ref.shape[1]
    lanes = held.shape[2]
    for copy in loads[:4]:
        copy.wait()
    page_hot = (
        lax.broadcasted_iota(jnp.int32, (lanes, pairs), 0) == pair_page_ref[...]
    ).astype(jnp.float32)
    query_hot = lax.broadcasted_iota(jnp.int32, (local_queries, pairs), 0) == pair_query_ref[...]
    counted = query_hot.astype(jnp.float32)
    labelled = counted * pair_label_ref[...].astype(jnp.float32)
    stacked = jnp.concatenate([counted, labelled], axis=0)
    flags = lax.dot_general(
        stacked, page_hot, (((1,), (1,)), ((), ())), preferred_element_type=jnp.float32
    )
    held[my_line, pl.ds(rows, flag_rows), :] = flags.astype(jnp.bfloat16)
    for step in range(1, lines):
        flags_to(my_line ^ step).start()

    offset = -0.5 * tokens_each * (math.log(patches) / 4.0 + 2.0)

    row_query = lax.broadcasted_iota(jnp.int32, (rows, flag_rows), 0) // tokens_each
    flag_row = lax.broadcasted_iota(jnp.int32, (rows, flag_rows), 1)
    count_pick = (flag_row == row_query).astype(jnp.bfloat16)
    label_pick = (flag_row == row_query + local_queries).astype(jnp.bfloat16)
    lane = lax.broadcasted_iota(jnp.int32, (1, lanes), 1)
    scale = 4.0 * math.log2(math.e)

    def logits(line, plane):
        return lax.dot_general(
            held[line, pl.ds(0, rows), :],
            paged[plane].reshape(patches, width),
            (((1,), (1,)), ((), ())),
            preferred_element_type=jnp.float32,
        )

    def weights(dots, line, plane):
        page = my_line * planes + plane
        own_lane = (lane == page).astype(jnp.float32)
        own_shift = 2.0 * jnp.sum((hot_ref[...] == page).astype(jnp.float32), keepdims=True)
        flag = held[line, pl.ds(rows, flag_rows), :]
        counts = jnp.sum(
            jnp.dot(count_pick, flag, preferred_element_type=jnp.float32) * own_lane,
            axis=1,
            keepdims=True,
        )
        labels = jnp.sum(
            jnp.dot(label_pick, flag, preferred_element_type=jnp.float32) * own_lane,
            axis=1,
            keepdims=True,
        )
        peak = jnp.max(dots, axis=1, keepdims=True)
        expo = jnp.exp2((dots - peak) * scale)
        totals = jnp.sum(expo, axis=1, keepdims=True)
        log_total = 4.0 * peak + jnp.log(totals)
        score = jnp.sum(log_total.reshape(local_queries, tokens_each, 1), axis=1, keepdims=True)
        score = jnp.broadcast_to(score, (local_queries, tokens_each, 1)).reshape(rows, 1)
        logit = 0.5 * (score / 4.0) + offset - own_shift
        slope = 0.5 * (counts * jax.nn.sigmoid(logit) - labels)
        return (expo * (slope / totals)).astype(jnp.bfloat16)

    started_lines, started_pages = set(), set()

    def gradients(weight, line, plane, first_line, first_page):
        tokens = held[line, pl.ds(0, rows), :]
        by_query = jnp.dot(
            weight, paged[plane].reshape(patches, width), preferred_element_type=jnp.float32
        )
        by_page = lax.dot_general(
            tokens, weight, (((0,), (0,)), ((), ())), preferred_element_type=jnp.float32
        )
        query_acc[line] = by_query if first_line else query_acc[line] + by_query
        for side in range(page_acc.shape[1]):
            terms = by_page[:, side * part : (side + 1) * part]
            page_acc[plane, side] = terms if first_page else page_acc[plane, side] + terms

    def block(*places):
        spots = [(my_line ^ hop, turn(jump)) for hop, jump in places]
        dots = [logits(*spot) for spot in spots]
        for spot, dot, (hop, jump) in zip(spots, dots, places):
            fresh = hop not in started_lines, jump not in started_pages
            started_lines.add(hop)
            started_pages.add(jump)
            gradients(weights(dot, *spot), *spot, *fresh)

    def half_page(plane):
        swap(plane).wait_recv()
        return page_acc[plane, core] + swap_in[plane].astype(jnp.float32)

    def act(kind, *what):
        if kind == "block":
            block(*what)
            return
        offset_by = what[0]
        line, plane = my_line ^ offset_by, turn(offset_by)
        if kind == "tokens":
            tokens_from(line).wait_recv()
            flags_from(line).wait_recv()
        elif kind == "send_tokens":
            tokens_to(line).start()
        elif kind == "sent_tokens":
            tokens_to(line).wait_send()
        elif kind == "send_page":
            page_on().start()
        elif kind == "sent_page":
            page_to(plane).wait_send()
        elif kind == "page":
            if offset_by < 3:
                page_from(plane, 1 - core).wait_recv()
            page_from(plane, core).wait_recv()
            relay(offset_by).start()
        elif kind == "relayed":
            relayed(offset_by).wait_recv()
        elif kind == "line":
            part_out[line] = query_acc[line].astype(jnp.bfloat16)
            part_to(line).start()
        elif kind == "finish":
            swap_out[plane] = page_acc[plane, 1 - core].astype(jnp.bfloat16)
            swap(plane).start()
        elif kind == "share":
            share_out[plane] = half_page(plane).astype(jnp.bfloat16)
            share_to(plane).start()

    block((0, 0))
    for step in plan():
        act(*step)

    total = query_acc[my_line]
    for step in range(1, lines):
        part_from(my_line ^ step).wait_recv()
        total += part_in[my_line ^ step].astype(jnp.float32)
    query_grad_ref[...] = total.astype(jnp.bfloat16)

    total = half_page(my_plane)
    for step in range(1, planes):
        share_from(my_plane ^ step).wait_recv()
        total += share_in[my_plane ^ step].astype(jnp.float32)
    page_grad_ref[...] = total.T.astype(jnp.bfloat16)

    swap(my_plane).wait_send()
    for step in range(1, lines):
        flags_to(my_line ^ step).wait_send()
        part_to(my_line ^ step).wait_send()
    for step in range(1, planes):
        plane = my_plane ^ step
        swap(plane).wait_send()
        share_to(plane).wait_send()
    relay(1).wait_send()
    relay(3).wait_send()
    tokens_to(my_line ^ 1).wait_send()
    tokens_to(my_line ^ 2).wait_send()
    tokens_to(my_line ^ 3).wait_send()
    page_to(1).wait_send()
    page_to(2).wait_send()
    page_on().wait_send()


def store_kernel(query_ref, page_ref, query_out, page_out, sems):
    copies = [
        pltpu.make_async_copy(query_ref, query_out, sems.at[0]),
        pltpu.make_async_copy(page_ref, page_out, sems.at[1]),
    ]
    for copy in copies:
        copy.start()
    for copy in copies:
        copy.wait()


def dense_shards(queries, pages, pair_page, pair_query, pair_label, hot_pages):
    owners = lax.axis_size("owner")
    replicas = lax.axis_size("replica")
    local_queries, tokens_each, width = queries.shape
    patches = pages.shape[1]
    pairs = pair_query.shape[0]
    rows = local_queries * tokens_each
    flag_rows = 2 * local_queries
    part = patches // replicas
    planes = math.isqrt(owners)
    lines = owners // planes
    vmem = pl.BlockSpec(memory_space=pltpu.VMEM)
    hbm = pl.BlockSpec(memory_space=pltpu.HBM)
    query_grad, page_grad = pl.pallas_call(
        functools.partial(
            dense_kernel, lines, planes, (local_queries, tokens_each, width, patches)
        ),
        out_shape=(
            jax.ShapeDtypeStruct((rows, width), jnp.bfloat16),
            jax.ShapeDtypeStruct((part, width), jnp.bfloat16),
        ),
        in_specs=[hbm] * 6,
        out_specs=(vmem, vmem),
        scratch_shapes=[
            *[pltpu.VMEM((1, pairs), jnp.int32)] * 3,
            pltpu.VMEM((1, hot_pages.shape[0]), jnp.int32),
            pltpu.VMEM((lines, rows + flag_rows, width), jnp.bfloat16),
            pltpu.VMEM((planes, replicas, part, width), jnp.bfloat16),
            pltpu.VMEM((planes, replicas, width, part), jnp.float32),
            pltpu.VMEM((lines, rows, width), jnp.float32),
            *[pltpu.VMEM((planes, width, part), jnp.bfloat16)] * 4,
            *[pltpu.VMEM((lines, rows, width), jnp.bfloat16)] * 2,
            pltpu.SemaphoreType.DMA((6,)),
            *[pltpu.SemaphoreType.DMA((lines,))] * 4,
            pltpu.SemaphoreType.DMA((planes,)),
            pltpu.SemaphoreType.DMA((planes, replicas)),
            *[pltpu.SemaphoreType.DMA((planes,))] * 6,
            *[pltpu.SemaphoreType.DMA((lines,))] * 2,
        ],
        compiler_params=pltpu.CompilerParams(
            collective_id=0, has_side_effects=True, vmem_limit_bytes=24 << 20
        ),
    )(
        *[
            pltpu.with_memory_space_constraint(operand, pltpu.HBM)
            for operand in (
                queries.reshape(rows, width),
                pages[0].reshape(replicas, part, width),
                pair_page.reshape(1, pairs),
                pair_query.reshape(1, pairs),
                pair_label.reshape(1, pairs),
                hot_pages.reshape(1, hot_pages.shape[0]),
            )
        ]
    )
    query_grad, page_grad = pl.pallas_call(
        store_kernel,
        out_shape=(
            jax.ShapeDtypeStruct(query_grad.shape, query_grad.dtype),
            jax.ShapeDtypeStruct(page_grad.shape, page_grad.dtype),
        ),
        in_specs=[vmem, vmem],
        out_specs=(hbm, hbm),
        scratch_shapes=[pltpu.SemaphoreType.DMA((2,))],
        compiler_params=pltpu.CompilerParams(vmem_limit_bytes=1 << 20),
    )(query_grad, page_grad)
    return query_grad.reshape(queries.shape), page_grad[None]


SHARPNESS = 4.0
SLOPE_SCALE = 0.5
HOT_SHIFT = 2.0


def score_block(token_rows, label_rows, page_rows, offset, shift):
    count = token_rows.shape[0]
    tokens_each = token_rows.shape[1]
    flat_rows = token_rows.reshape(count * tokens_each, token_rows.shape[2])
    logits = SHARPNESS * lax.dot_general(
        flat_rows, page_rows, (((1,), (1,)), ((), ())), preferred_element_type=jnp.float32
    )
    peak = jnp.max(logits, axis=1, keepdims=True)
    expo = jnp.exp(logits - peak)
    totals = jnp.sum(expo, axis=1, keepdims=True)
    log_total = peak + jnp.log(totals)
    score = jnp.sum(log_total.reshape(count, tokens_each), axis=1) / SHARPNESS
    logit = SLOPE_SCALE * score + offset - shift
    slope = SLOPE_SCALE * (jax.nn.sigmoid(logit) - label_rows[:, 0]) * label_rows[:, 1]
    slope_rows = jnp.repeat(slope, tokens_each)[:, None]
    weight = (expo / totals * slope_rows).astype(jnp.bfloat16)
    grads = jnp.dot(weight, page_rows, preferred_element_type=jnp.float32).astype(jnp.bfloat16)
    page_part = lax.dot_general(
        weight, flat_rows, (((0,), (0,)), ((), ())), preferred_element_type=jnp.float32
    )
    return (grads.reshape(token_rows.shape), page_part)


def sparse_shards(queries, pages, pair_page, pair_query, pair_label, hot_pages):
    owners = lax.axis_size("owner")
    owner_place = lax.axis_index("owner")
    local_pairs = pair_page.shape[0]
    local_queries = queries.shape[0]
    tokens_each = queries.shape[1]
    width = queries.shape[2]
    patch_count = pages.shape[1]
    capacity = max(2, 4 * local_pairs // owners)
    slots = owners * capacity
    offset = -SLOPE_SCALE * tokens_each * (math.log(patch_count) / SHARPNESS + SHARPNESS / 2.0)
    targets = pair_page[:, 0]
    owned_hot = (hot_pages == owner_place).astype(jnp.float32)
    target_hot = (targets[:, None] == jnp.arange(owners, dtype=jnp.int32)[None, :]).astype(
        jnp.int32
    )
    earlier = jnp.cumsum(target_hot, axis=0) - target_hot
    rank_within = jnp.sum(earlier * target_hot, axis=1)
    slot_of = targets * capacity + rank_within
    select = (slot_of[None, :] == jnp.arange(slots, dtype=jnp.int32)[:, None]).astype(jnp.bfloat16)
    query_hot = (pair_query[:, None] == jnp.arange(local_queries, dtype=jnp.int32)[None, :]).astype(
        jnp.bfloat16
    )
    pair_tokens = jnp.dot(
        query_hot,
        queries.reshape(local_queries, tokens_each * width),
        preferred_element_type=jnp.float32,
    ).astype(jnp.bfloat16)
    send_tokens = jnp.dot(select, pair_tokens, preferred_element_type=jnp.float32).astype(
        jnp.bfloat16
    )
    pair_flags = jnp.stack(
        [pair_label.astype(jnp.float32), jnp.ones((local_pairs,), jnp.float32)], axis=1
    ).astype(jnp.bfloat16)
    send_flags = jnp.dot(select, pair_flags, preferred_element_type=jnp.float32).astype(
        jnp.bfloat16
    )
    got_tokens, got_flags = (
        lax.all_to_all(
            send_tokens.reshape(owners, capacity * tokens_each * width),
            "owner",
            split_axis=0,
            concat_axis=0,
            tiled=True,
        ),
        lax.all_to_all(
            send_flags.reshape(owners, capacity * 2),
            "owner",
            split_axis=0,
            concat_axis=0,
            tiled=True,
        ),
    )
    slot_tokens = got_tokens.reshape(slots, tokens_each, width)
    slot_flags = got_flags.reshape(slots, 2).astype(jnp.float32)
    page_rows = pages[0]
    own_shift = HOT_SHIFT * jnp.sum(owned_hot)
    block_rows = slots // max(1, slots // 64)
    filled = (slot_flags[:, 1] > 0.5).astype(jnp.int32)
    order = jnp.argsort(1 - filled, stable=True)
    inverse = jnp.argsort(order, stable=True)
    sorted_tokens = slot_tokens[order]
    sorted_flags = slot_flags[order]
    live_blocks = (jnp.sum(filled) + block_rows - 1) // block_rows

    def visit(block_id, carry):
        grad_store, page_acc = carry
        start = (block_id * block_rows).astype(jnp.int32)
        token_rows = lax.dynamic_slice_in_dim(sorted_tokens, start, block_rows, 0)
        label_rows = lax.dynamic_slice_in_dim(sorted_flags, start, block_rows, 0)
        grads, page_part = score_block(token_rows, label_rows, page_rows, offset, own_shift)
        grad_store = lax.dynamic_update_slice_in_dim(grad_store, grads, start, 0)
        return (grad_store, page_acc + page_part)

    sorted_grads, page_terms = lax.fori_loop(
        0,
        live_blocks,
        visit,
        (
            jnp.zeros((slots, tokens_each, width), jnp.bfloat16),
            jnp.zeros((patch_count, width), jnp.float32),
        ),
    )
    slot_grads = sorted_grads[inverse]
    returned = lax.all_to_all(
        slot_grads.reshape(owners, capacity * tokens_each * width),
        "owner",
        split_axis=0,
        concat_axis=0,
        tiled=True,
    )
    pair_grads = lax.dot_general(
        select,
        returned.reshape(slots, tokens_each * width),
        (((0,), (0,)), ((), ())),
        preferred_element_type=jnp.float32,
    )
    summed = lax.dot_general(
        query_hot.astype(jnp.float32),
        pair_grads,
        (((0,), (0,)), ((), ())),
        precision=lax.Precision.HIGHEST,
        preferred_element_type=jnp.float32,
    )
    query_grad = summed.reshape(local_queries, tokens_each, width).astype(jnp.bfloat16)
    page_share = lax.psum_scatter(
        page_terms.astype(jnp.bfloat16), "replica", scatter_dimension=0, tiled=True
    )
    return (query_grad, page_share[None])


def shards(queries, pages, pair_page, pair_query, pair_label, hot_pages):
    owners = lax.axis_size("owner")
    replicas = lax.axis_size("replica")
    local_pairs = pair_query.shape[0]
    local_queries = queries.shape[0]
    capacity = max(2, 4 * local_pairs // owners)
    dense = capacity >= local_queries and owners <= queries.shape[2] and replicas == 2
    dense = dense and owners == len(ORDER) ** 2
    plan = dense_shards if dense else sparse_shards
    return plan(queries, pages, pair_page, pair_query, pair_label, hot_pages)


def solution(mesh):
    placed = (
        P(("owner", "replica"), None, None),
        P("owner", None, None),
        P(("owner", "replica"), None),
        P(("owner", "replica")),
        P(("owner", "replica")),
        P(),
    )
    return jax.shard_map(
        shards,
        mesh=mesh,
        in_specs=placed,
        out_specs=(P(("owner", "replica"), None, None), P("owner", "replica", None)),
        check_vma=False,
    )
```

```python
import functools
import math

import jax
import jax.numpy as jnp
from jax import lax
from jax.experimental import pallas as pl
from jax.experimental.pallas import tpu as pltpu
from jax.sharding import PartitionSpec as P

MESH = pl.DeviceIdType.MESH


ORDER = range(4)

def plan():
    return (
        ("tokens", 1),
        ("block", (1, 0)),
        ("page", 1),
        ("send_page", 3),
        ("send_tokens", 2),
        ("block", (0, 1), (1, 1)),
        ("tokens", 3),
        ("relayed", 2),
        ("block", (3, 1), (3, 0), (0, 2), (1, 2), (3, 2)),
        ("page", 3),
        ("tokens", 2),
        ("block", (2, 1), (2, 2)),
        ("finish", 1),
        ("finish", 2),
        ("relayed", 3),
        ("block", (3, 3), (1, 3)),
        ("line", 3),
        ("line", 1),
        ("share", 1),
        ("share", 2),
        ("block", (2, 3), (0, 3)),
        ("finish", 3),
        ("block", (2, 0)),
        ("line", 2),
        ("share", 3),
        ("finish", 0),
    )


def dense_kernel(
    lines,
    planes,
    shapes,
    query_ref,
    page_ref,
    pair_page_hbm,
    pair_query_hbm,
    pair_label_hbm,
    hot_hbm,
    query_grad_ref,
    page_grad_ref,
    pair_page_ref,
    pair_query_ref,
    pair_label_ref,
    hot_ref,
    held,
    paged,
    page_acc,
    query_acc,
    swap_out,
    swap_in,
    share_out,
    share_in,
    part_out,
    part_in,
    load_sem,
    line_sem,
    line_in_sem,
    flag_sem,
    flag_in_sem,
    plane_sem,
    plane_in_sem,
    relay_sem,
    relay_in_sem,
    swap_sem,
    swap_in_sem,
    share_sem,
    share_in_sem,
    part_sem,
    part_in_sem,
):
    local_queries, tokens_each, width, patches = shapes
    rows = local_queries * tokens_each
    flag_rows = held.shape[1] - rows
    part = page_acc.shape[3]
    me = lax.axis_index("owner")
    core = lax.axis_index("replica")
    my_line, my_plane = me // planes, me % planes

    def load(src, dst, place):
        return pltpu.make_async_copy(src, dst, load_sem.at[place])

    loads = [
        load(pair_page_hbm, pair_page_ref, 0),
        load(pair_query_hbm, pair_query_ref, 1),
        load(pair_label_hbm, pair_label_ref, 2),
        load(hot_hbm, hot_ref, 3),
        load(query_ref, held.at[my_line, pl.ds(0, rows), :], 4),
        load(page_ref, paged.at[my_plane], 5),
    ]

    barrier = pltpu.get_barrier_semaphore()

    def greet(owner):
        pl.semaphore_signal(barrier, inc=1, device_id={"owner": owner}, device_id_type=MESH)

    for step in range(1, lines):
        greet((my_line ^ step) * planes + my_plane)
    for step in range(1, planes):
        greet(my_line * planes + (my_plane ^ step))
    pl.semaphore_signal(barrier, inc=1, device_id={"replica": 1 - core}, device_id_type=MESH)
    across = {"owner": my_line * planes + (my_plane ^ (1 + core)), "replica": 1 - core}
    pl.semaphore_signal(barrier, inc=1, device_id=across, device_id_type=MESH)
    for copy in loads:
        copy.start()

    def remote(src, dst, sent, received, device):
        return pltpu.make_async_remote_copy(
            src_ref=src,
            dst_ref=dst,
            send_sem=sent,
            recv_sem=received,
            device_id=device,
            device_id_type=MESH,
        )

    def to_line(line):
        return {"owner": line * planes + my_plane}

    def to_plane(plane):
        return {"owner": my_line * planes + plane}

    twin = {"replica": 1 - core}

    def tokens_to(line):
        slot = held.at[my_line, pl.ds(0, rows), :]
        return remote(slot, slot, line_sem.at[line], line_in_sem.at[my_line], to_line(line))

    def tokens_from(line):
        slot = held.at[line, pl.ds(0, rows), :]
        return remote(slot, slot, line_sem.at[line], line_in_sem.at[line], to_line(line))

    def flags_to(line):
        slot = held.at[my_line, pl.ds(rows, flag_rows), :]
        return remote(slot, slot, flag_sem.at[line], flag_in_sem.at[my_line], to_line(line))

    def flags_from(line):
        slot = held.at[line, pl.ds(rows, flag_rows), :]
        return remote(slot, slot, flag_sem.at[line], flag_in_sem.at[line], to_line(line))

    def turn(jump):
        return my_plane ^ (0, 1 + core, 2 - core, 3)[jump]

    def page_to(jump):
        slot = paged.at[my_plane, core]
        plane = my_plane ^ jump
        device = {"owner": my_line * planes + plane, "replica": jump - 1}
        return remote(slot, slot, plane_sem.at[plane], plane_in_sem.at[my_plane, core], device)

    def page_on():
        slot = paged.at[turn(1), core]
        sent, received = plane_sem.at[turn(3)], plane_in_sem.at[turn(1), core]
        return remote(slot, slot, sent, received, to_plane(turn(2)))

    def page_from(plane, side):
        slot = paged.at[plane, side]
        sent, received = plane_sem.at[plane], plane_in_sem.at[plane, side]
        return remote(slot, slot, sent, received, to_plane(plane))

    def relay(jump):
        plane = turn(jump)
        slot = paged.at[plane] if jump < 3 else paged.at[plane, core]
        return remote(slot, slot, relay_sem.at[plane], relay_in_sem.at[plane], twin)

    def relayed(jump):
        plane = turn(jump)
        slot = paged.at[plane] if jump < 3 else paged.at[plane, 1 - core]
        return remote(slot, slot, relay_sem.at[plane], relay_in_sem.at[plane], twin)

    def swap(plane):
        return remote(
            swap_out.at[plane], swap_in.at[plane], swap_sem.at[plane], swap_in_sem.at[plane], twin
        )

    def share_to(plane):
        dst = share_in.at[my_plane]
        sent, received = share_sem.at[plane], share_in_sem.at[my_plane]
        return remote(share_out.at[plane], dst, sent, received, to_plane(plane))

    def share_from(plane):
        dst = share_in.at[plane]
        sent, received = share_sem.at[plane], share_in_sem.at[plane]
        return remote(share_out.at[plane], dst, sent, received, to_plane(plane))

    def part_to(line):
        dst = part_in.at[my_line]
        sent, received = part_sem.at[line], part_in_sem.at[my_line]
        return remote(part_out.at[line], dst, sent, received, to_line(line))

    def part_from(line):
        dst = part_in.at[line]
        sent, received = part_sem.at[line], part_in_sem.at[line]
        return remote(part_out.at[line], dst, sent, received, to_line(line))

    loads[4].wait()
    loads[5].wait()
    pl.semaphore_wait(barrier, lines + planes)
    page_to(1).start()
    page_to(2).start()
    tokens_to(my_line ^ 1).start()
    tokens_to(my_line ^ 3).start()

    pairs = pair_page_ref.shape[1]
    lanes = held.shape[2]
    for copy in loads[:4]:
        copy.wait()
    page_hot = (
        lax.broadcasted_iota(jnp.int32, (lanes, pairs), 0) == pair_page_ref[...]
    ).astype(jnp.float32)
    query_hot = lax.broadcasted_iota(jnp.int32, (local_queries, pairs), 0) == pair_query_ref[...]
    counted = query_hot.astype(jnp.float32)
    labelled = counted * pair_label_ref[...].astype(jnp.float32)
    stacked = jnp.concatenate([counted, labelled], axis=0)
    flags = lax.dot_general(
        stacked, page_hot, (((1,), (1,)), ((), ())), preferred_element_type=jnp.float32
    )
    held[my_line, pl.ds(rows, flag_rows), :] = flags.astype(jnp.bfloat16)
    for step in range(1, lines):
        flags_to(my_line ^ step).start()

    offset = -0.5 * tokens_each * (math.log(patches) / 4.0 + 2.0)

    row_query = lax.broadcasted_iota(jnp.int32, (rows, flag_rows), 0) // tokens_each
    flag_row = lax.broadcasted_iota(jnp.int32, (rows, flag_rows), 1)
    count_pick = (flag_row == row_query).astype(jnp.bfloat16)
    label_pick = (flag_row == row_query + local_queries).astype(jnp.bfloat16)
    lane = lax.broadcasted_iota(jnp.int32, (1, lanes), 1)
    scale = 4.0 * math.log2(math.e)

    def logits(line, plane):
        return lax.dot_general(
            held[line, pl.ds(0, rows), :],
            paged[plane].reshape(patches, width),
            (((1,), (1,)), ((), ())),
            preferred_element_type=jnp.float32,
        )

    def weights(dots, line, plane):
        page = my_line * planes + plane
        own_lane = (lane == page).astype(jnp.float32)
        own_shift = 2.0 * jnp.sum((hot_ref[...] == page).astype(jnp.float32), keepdims=True)
        flag = held[line, pl.ds(rows, flag_rows), :]
        counts = jnp.sum(
            jnp.dot(count_pick, flag, preferred_element_type=jnp.float32) * own_lane,
            axis=1,
            keepdims=True,
        )
        labels = jnp.sum(
            jnp.dot(label_pick, flag, preferred_element_type=jnp.float32) * own_lane,
            axis=1,
            keepdims=True,
        )
        peak = jnp.max(dots, axis=1, keepdims=True)
        expo = jnp.exp2((dots - peak) * scale)
        totals = jnp.sum(expo, axis=1, keepdims=True)
        log_total = 4.0 * peak + jnp.log(totals)
        score = jnp.sum(log_total.reshape(local_queries, tokens_each, 1), axis=1, keepdims=True)
        score = jnp.broadcast_to(score, (local_queries, tokens_each, 1)).reshape(rows, 1)
        logit = 0.5 * (score / 4.0) + offset - own_shift
        slope = 0.5 * (counts * jax.nn.sigmoid(logit) - labels)
        return (expo * (slope / totals)).astype(jnp.bfloat16)

    started_lines, started_pages = set(), set()

    def gradients(weight, line, plane, first_line, first_page):
        tokens = held[line, pl.ds(0, rows), :]
        by_query = jnp.dot(
            weight, paged[plane].reshape(patches, width), preferred_element_type=jnp.float32
        )
        by_page = lax.dot_general(
            tokens, weight, (((0,), (0,)), ((), ())), preferred_element_type=jnp.float32
        )
        query_acc[line] = by_query if first_line else query_acc[line] + by_query
        for side in range(page_acc.shape[1]):
            terms = by_page[:, side * part : (side + 1) * part]
            page_acc[plane, side] = terms if first_page else page_acc[plane, side] + terms

    def block(*places):
        spots = [(my_line ^ hop, turn(jump)) for hop, jump in places]
        dots = [logits(*spot) for spot in spots]
        for spot, dot, (hop, jump) in zip(spots, dots, places):
            fresh = hop not in started_lines, jump not in started_pages
            started_lines.add(hop)
            started_pages.add(jump)
            gradients(weights(dot, *spot), *spot, *fresh)

    def half_page(plane):
        swap(plane).wait_recv()
        return page_acc[plane, core] + swap_in[plane].astype(jnp.float32)

    def act(kind, *what):
        if kind == "block":
            block(*what)
            return
        offset_by = what[0]
        line, plane = my_line ^ offset_by, turn(offset_by)
        if kind == "tokens":
            tokens_from(line).wait_recv()
            flags_from(line).wait_recv()
        elif kind == "send_tokens":
            tokens_to(line).start()
        elif kind == "sent_tokens":
            tokens_to(line).wait_send()
        elif kind == "send_page":
            page_on().start()
        elif kind == "sent_page":
            page_to(plane).wait_send()
        elif kind == "page":
            if offset_by < 3:
                page_from(plane, 1 - core).wait_recv()
            page_from(plane, core).wait_recv()
            relay(offset_by).start()
        elif kind == "relayed":
            relayed(offset_by).wait_recv()
        elif kind == "line":
            part_out[line] = query_acc[line].astype(jnp.bfloat16)
            part_to(line).start()
        elif kind == "finish":
            swap_out[plane] = page_acc[plane, 1 - core].astype(jnp.bfloat16)
            swap(plane).start()
        elif kind == "share":
            share_out[plane] = half_page(plane).astype(jnp.bfloat16)
            share_to(plane).start()

    block((0, 0))
    for step in plan():
        act(*step)

    total = query_acc[my_line]
    for step in range(1, lines):
        part_from(my_line ^ step).wait_recv()
        total += part_in[my_line ^ step].astype(jnp.float32)
    query_grad_ref[...] = total.astype(jnp.bfloat16)

    total = half_page(my_plane)
    for step in range(1, planes):
        share_from(my_plane ^ step).wait_recv()
        total += share_in[my_plane ^ step].astype(jnp.float32)
    page_grad_ref[...] = total.T.astype(jnp.bfloat16)

    swap(my_plane).wait_send()
    for step in range(1, lines):
        flags_to(my_line ^ step).wait_send()
        part_to(my_line ^ step).wait_send()
    for step in range(1, planes):
        plane = my_plane ^ step
        swap(plane).wait_send()
        share_to(plane).wait_send()
    relay(1).wait_send()
    relay(3).wait_send()
    tokens_to(my_line ^ 1).wait_send()
    tokens_to(my_line ^ 2).wait_send()
    tokens_to(my_line ^ 3).wait_send()
    page_to(1).wait_send()
    page_to(2).wait_send()
    page_on().wait_send()


def store_kernel(query_ref, page_ref, query_out, page_out, sems):
    copies = [
        pltpu.make_async_copy(query_ref, query_out, sems.at[0]),
        pltpu.make_async_copy(page_ref, page_out, sems.at[1]),
    ]
    for copy in copies:
        copy.start()
    for copy in copies:
        copy.wait()


def dense_shards(queries, pages, pair_page, pair_query, pair_label, hot_pages):
    owners = lax.axis_size("owner")
    replicas = lax.axis_size("replica")
    local_queries, tokens_each, width = queries.shape
    patches = pages.shape[1]
    pairs = pair_query.shape[0]
    rows = local_queries * tokens_each
    flag_rows = 2 * local_queries
    part = patches // replicas
    planes = math.isqrt(owners)
    lines = owners // planes
    vmem = pl.BlockSpec(memory_space=pltpu.VMEM)
    hbm = pl.BlockSpec(memory_space=pltpu.HBM)
    query_grad, page_grad = pl.pallas_call(
        functools.partial(
            dense_kernel, lines, planes, (local_queries, tokens_each, width, patches)
        ),
        out_shape=(
            jax.ShapeDtypeStruct((rows, width), jnp.bfloat16),
            jax.ShapeDtypeStruct((part, width), jnp.bfloat16),
        ),
        in_specs=[hbm] * 6,
        out_specs=(vmem, vmem),
        scratch_shapes=[
            *[pltpu.VMEM((1, pairs), jnp.int32)] * 3,
            pltpu.VMEM((1, hot_pages.shape[0]), jnp.int32),
            pltpu.VMEM((lines, rows + flag_rows, width), jnp.bfloat16),
            pltpu.VMEM((planes, replicas, part, width), jnp.bfloat16),
            pltpu.VMEM((planes, replicas, width, part), jnp.float32),
            pltpu.VMEM((lines, rows, width), jnp.float32),
            *[pltpu.VMEM((planes, width, part), jnp.bfloat16)] * 4,
            *[pltpu.VMEM((lines, rows, width), jnp.bfloat16)] * 2,
            pltpu.SemaphoreType.DMA((6,)),
            *[pltpu.SemaphoreType.DMA((lines,))] * 4,
            pltpu.SemaphoreType.DMA((planes,)),
            pltpu.SemaphoreType.DMA((planes, replicas)),
            *[pltpu.SemaphoreType.DMA((planes,))] * 6,
            *[pltpu.SemaphoreType.DMA((lines,))] * 2,
        ],
        compiler_params=pltpu.CompilerParams(
            collective_id=0, has_side_effects=True, vmem_limit_bytes=24 << 20
        ),
    )(
        *[
            pltpu.with_memory_space_constraint(operand, pltpu.HBM)
            for operand in (
                queries.reshape(rows, width),
                pages[0].reshape(replicas, part, width),
                pair_page.reshape(1, pairs),
                pair_query.reshape(1, pairs),
                pair_label.reshape(1, pairs),
                hot_pages.reshape(1, hot_pages.shape[0]),
            )
        ]
    )
    query_grad, page_grad = pl.pallas_call(
        store_kernel,
        out_shape=(
            jax.ShapeDtypeStruct(query_grad.shape, query_grad.dtype),
            jax.ShapeDtypeStruct(page_grad.shape, page_grad.dtype),
        ),
        in_specs=[vmem, vmem],
        out_specs=(hbm, hbm),
        scratch_shapes=[pltpu.SemaphoreType.DMA((2,))],
        compiler_params=pltpu.CompilerParams(vmem_limit_bytes=1 << 20),
    )(query_grad, page_grad)
    return query_grad.reshape(queries.shape), page_grad[None]


SHARPNESS = 4.0
SLOPE_SCALE = 0.5
HOT_SHIFT = 2.0


def score_block(token_rows, label_rows, page_rows, offset, shift):
    count = token_rows.shape[0]
    tokens_each = token_rows.shape[1]
    flat_rows = token_rows.reshape(count * tokens_each, token_rows.shape[2])
    logits = SHARPNESS * lax.dot_general(
        flat_rows, page_rows, (((1,), (1,)), ((), ())), preferred_element_type=jnp.float32
    )
    peak = jnp.max(logits, axis=1, keepdims=True)
    expo = jnp.exp(logits - peak)
    totals = jnp.sum(expo, axis=1, keepdims=True)
    log_total = peak + jnp.log(totals)
    score = jnp.sum(log_total.reshape(count, tokens_each), axis=1) / SHARPNESS
    logit = SLOPE_SCALE * score + offset - shift
    slope = SLOPE_SCALE * (jax.nn.sigmoid(logit) - label_rows[:, 0]) * label_rows[:, 1]
    slope_rows = jnp.repeat(slope, tokens_each)[:, None]
    weight = (expo / totals * slope_rows).astype(jnp.bfloat16)
    grads = jnp.dot(weight, page_rows, preferred_element_type=jnp.float32).astype(jnp.bfloat16)
    page_part = lax.dot_general(
        weight, flat_rows, (((0,), (0,)), ((), ())), preferred_element_type=jnp.float32
    )
    return (grads.reshape(token_rows.shape), page_part)


def sparse_shards(queries, pages, pair_page, pair_query, pair_label, hot_pages):
    owners = lax.axis_size("owner")
    owner_place = lax.axis_index("owner")
    local_pairs = pair_page.shape[0]
    local_queries = queries.shape[0]
    tokens_each = queries.shape[1]
    width = queries.shape[2]
    patch_count = pages.shape[1]
    capacity = max(2, 4 * local_pairs // owners)
    slots = owners * capacity
    offset = -SLOPE_SCALE * tokens_each * (math.log(patch_count) / SHARPNESS + SHARPNESS / 2.0)
    targets = pair_page[:, 0]
    owned_hot = (hot_pages == owner_place).astype(jnp.float32)
    target_hot = (targets[:, None] == jnp.arange(owners, dtype=jnp.int32)[None, :]).astype(
        jnp.int32
    )
    earlier = jnp.cumsum(target_hot, axis=0) - target_hot
    rank_within = jnp.sum(earlier * target_hot, axis=1)
    slot_of = targets * capacity + rank_within
    select = (slot_of[None, :] == jnp.arange(slots, dtype=jnp.int32)[:, None]).astype(jnp.bfloat16)
    query_hot = (pair_query[:, None] == jnp.arange(local_queries, dtype=jnp.int32)[None, :]).astype(
        jnp.bfloat16
    )
    pair_tokens = jnp.dot(
        query_hot,
        queries.reshape(local_queries, tokens_each * width),
        preferred_element_type=jnp.float32,
    ).astype(jnp.bfloat16)
    send_tokens = jnp.dot(select, pair_tokens, preferred_element_type=jnp.float32).astype(
        jnp.bfloat16
    )
    pair_flags = jnp.stack(
        [pair_label.astype(jnp.float32), jnp.ones((local_pairs,), jnp.float32)], axis=1
    ).astype(jnp.bfloat16)
    send_flags = jnp.dot(select, pair_flags, preferred_element_type=jnp.float32).astype(
        jnp.bfloat16
    )
    got_tokens, got_flags = (
        lax.all_to_all(
            send_tokens.reshape(owners, capacity * tokens_each * width),
            "owner",
            split_axis=0,
            concat_axis=0,
            tiled=True,
        ),
        lax.all_to_all(
            send_flags.reshape(owners, capacity * 2),
            "owner",
            split_axis=0,
            concat_axis=0,
            tiled=True,
        ),
    )
    slot_tokens = got_tokens.reshape(slots, tokens_each, width)
    slot_flags = got_flags.reshape(slots, 2).astype(jnp.float32)
    page_rows = pages[0]
    own_shift = HOT_SHIFT * jnp.sum(owned_hot)
    block_rows = slots // max(1, slots // 64)
    filled = (slot_flags[:, 1] > 0.5).astype(jnp.int32)
    order = jnp.argsort(1 - filled, stable=True)
    inverse = jnp.argsort(order, stable=True)
    sorted_tokens = slot_tokens[order]
    sorted_flags = slot_flags[order]
    live_blocks = (jnp.sum(filled) + block_rows - 1) // block_rows

    def visit(block_id, carry):
        grad_store, page_acc = carry
        start = (block_id * block_rows).astype(jnp.int32)
        token_rows = lax.dynamic_slice_in_dim(sorted_tokens, start, block_rows, 0)
        label_rows = lax.dynamic_slice_in_dim(sorted_flags, start, block_rows, 0)
        grads, page_part = score_block(token_rows, label_rows, page_rows, offset, own_shift)
        grad_store = lax.dynamic_update_slice_in_dim(grad_store, grads, start, 0)
        return (grad_store, page_acc + page_part)

    sorted_grads, page_terms = lax.fori_loop(
        0,
        live_blocks,
        visit,
        (
            jnp.zeros((slots, tokens_each, width), jnp.bfloat16),
            jnp.zeros((patch_count, width), jnp.float32),
        ),
    )
    slot_grads = sorted_grads[inverse]
    returned = lax.all_to_all(
        slot_grads.reshape(owners, capacity * tokens_each * width),
        "owner",
        split_axis=0,
        concat_axis=0,
        tiled=True,
    )
    pair_grads = lax.dot_general(
        select,
        returned.reshape(slots, tokens_each * width),
        (((0,), (0,)), ((), ())),
        preferred_element_type=jnp.float32,
    )
    summed = lax.dot_general(
        query_hot.astype(jnp.float32),
        pair_grads,
        (((0,), (0,)), ((), ())),
        precision=lax.Precision.HIGHEST,
        preferred_element_type=jnp.float32,
    )
    query_grad = summed.reshape(local_queries, tokens_each, width).astype(jnp.bfloat16)
    page_share = lax.psum_scatter(
        page_terms.astype(jnp.bfloat16), "replica", scatter_dimension=0, tiled=True
    )
    return (query_grad, page_share[None])


def shards(queries, pages, pair_page, pair_query, pair_label, hot_pages):
    owners = lax.axis_size("owner")
    replicas = lax.axis_size("replica")
    local_pairs = pair_query.shape[0]
    local_queries = queries.shape[0]
    capacity = max(2, 4 * local_pairs // owners)
    dense = capacity >= local_queries and owners <= queries.shape[2] and replicas == 2
    dense = dense and owners == len(ORDER) ** 2
    plan = dense_shards if dense else sparse_shards
    return plan(queries, pages, pair_page, pair_query, pair_label, hot_pages)


def solution(mesh):
    placed = (
        P(("owner", "replica"), None, None),
        P("owner", None, None),
        P(("owner", "replica"), None),
        P(("owner", "replica")),
        P(("owner", "replica")),
        P(),
    )
    return jax.shard_map(
        shards,
        mesh=mesh,
        in_specs=placed,
        out_specs=(P(("owner", "replica"), None, None), P("owner", "replica", None)),
        check_vma=False,
    )
```

```python
import functools
import math

import jax
import jax.numpy as jnp
from jax import lax
from jax.experimental import pallas as pl
from jax.experimental.pallas import tpu as pltpu
from jax.sharding import PartitionSpec as P

MESH = pl.DeviceIdType.MESH


ORDER = range(4)

def plan():
    return (
        ("tokens", 1),
        ("block", (1, 0)),
        ("send_tokens", 2),
        ("page", 1),
        ("send_page", 3),
        ("block", (0, 1), (1, 1)),
        ("tokens", 3),
        ("relayed", 2),
        ("block", (3, 1), (3, 0), (0, 2), (1, 2), (3, 2)),
        ("page", 3),
        ("tokens", 2),
        ("block", (2, 1), (2, 2)),
        ("finish", 1),
        ("finish", 2),
        ("relayed", 3),
        ("block", (3, 3), (1, 3)),
        ("line", 3),
        ("line", 1),
        ("share", 1),
        ("share", 2),
        ("block", (2, 3), (0, 3)),
        ("finish", 3),
        ("block", (2, 0)),
        ("line", 2),
        ("share", 3),
        ("finish", 0),
    )


def dense_kernel(
    lines,
    planes,
    shapes,
    query_ref,
    page_ref,
    pair_page_hbm,
    pair_query_hbm,
    pair_label_hbm,
    hot_hbm,
    query_grad_ref,
    page_grad_ref,
    pair_page_ref,
    pair_query_ref,
    pair_label_ref,
    hot_ref,
    held,
    paged,
    page_acc,
    query_acc,
    swap_out,
    swap_in,
    share_out,
    share_in,
    part_out,
    part_in,
    load_sem,
    line_sem,
    line_in_sem,
    flag_sem,
    flag_in_sem,
    plane_sem,
    plane_in_sem,
    relay_sem,
    relay_in_sem,
    swap_sem,
    swap_in_sem,
    share_sem,
    share_in_sem,
    part_sem,
    part_in_sem,
):
    local_queries, tokens_each, width, patches = shapes
    rows = local_queries * tokens_each
    flag_rows = held.shape[1] - rows
    part = page_acc.shape[3]
    me = lax.axis_index("owner")
    core = lax.axis_index("replica")
    my_line, my_plane = me // planes, me % planes

    def load(src, dst, place):
        return pltpu.make_async_copy(src, dst, load_sem.at[place])

    loads = [
        load(pair_page_hbm, pair_page_ref, 0),
        load(pair_query_hbm, pair_query_ref, 1),
        load(pair_label_hbm, pair_label_ref, 2),
        load(hot_hbm, hot_ref, 3),
        load(query_ref, held.at[my_line, pl.ds(0, rows), :], 4),
        load(page_ref, paged.at[my_plane], 5),
    ]

    barrier = pltpu.get_barrier_semaphore()

    def greet(owner):
        pl.semaphore_signal(barrier, inc=1, device_id={"owner": owner}, device_id_type=MESH)

    for step in range(1, lines):
        greet((my_line ^ step) * planes + my_plane)
    for step in range(1, planes):
        greet(my_line * planes + (my_plane ^ step))
    pl.semaphore_signal(barrier, inc=1, device_id={"replica": 1 - core}, device_id_type=MESH)
    across = {"owner": my_line * planes + (my_plane ^ (1 + core)), "replica": 1 - core}
    pl.semaphore_signal(barrier, inc=1, device_id=across, device_id_type=MESH)
    for copy in loads:
        copy.start()

    def remote(src, dst, sent, received, device):
        return pltpu.make_async_remote_copy(
            src_ref=src,
            dst_ref=dst,
            send_sem=sent,
            recv_sem=received,
            device_id=device,
            device_id_type=MESH,
        )

    def to_line(line):
        return {"owner": line * planes + my_plane}

    def to_plane(plane):
        return {"owner": my_line * planes + plane}

    twin = {"replica": 1 - core}

    def tokens_to(line):
        slot = held.at[my_line, pl.ds(0, rows), :]
        return remote(slot, slot, line_sem.at[line], line_in_sem.at[my_line], to_line(line))

    def tokens_from(line):
        slot = held.at[line, pl.ds(0, rows), :]
        return remote(slot, slot, line_sem.at[line], line_in_sem.at[line], to_line(line))

    def flags_to(line):
        slot = held.at[my_line, pl.ds(rows, flag_rows), :]
        return remote(slot, slot, flag_sem.at[line], flag_in_sem.at[my_line], to_line(line))

    def flags_from(line):
        slot = held.at[line, pl.ds(rows, flag_rows), :]
        return remote(slot, slot, flag_sem.at[line], flag_in_sem.at[line], to_line(line))

    def turn(jump):
        return my_plane ^ (0, 1 + core, 2 - core, 3)[jump]

    def page_to(jump):
        slot = paged.at[my_plane, core]
        plane = my_plane ^ jump
        device = {"owner": my_line * planes + plane, "replica": jump - 1}
        return remote(slot, slot, plane_sem.at[plane], plane_in_sem.at[my_plane, core], device)

    def page_on():
        slot = paged.at[turn(1), core]
        sent, received = plane_sem.at[turn(3)], plane_in_sem.at[turn(1), core]
        return remote(slot, slot, sent, received, to_plane(turn(2)))

    def page_from(plane, side):
        slot = paged.at[plane, side]
        sent, received = plane_sem.at[plane], plane_in_sem.at[plane, side]
        return remote(slot, slot, sent, received, to_plane(plane))

    def relay(jump):
        plane = turn(jump)
        slot = paged.at[plane] if jump < 3 else paged.at[plane, core]
        return remote(slot, slot, relay_sem.at[plane], relay_in_sem.at[plane], twin)

    def relayed(jump):
        plane = turn(jump)
        slot = paged.at[plane] if jump < 3 else paged.at[plane, 1 - core]
        return remote(slot, slot, relay_sem.at[plane], relay_in_sem.at[plane], twin)

    def swap(plane):
        return remote(
            swap_out.at[plane], swap_in.at[plane], swap_sem.at[plane], swap_in_sem.at[plane], twin
        )

    def share_to(plane):
        dst = share_in.at[my_plane]
        sent, received = share_sem.at[plane], share_in_sem.at[my_plane]
        return remote(share_out.at[plane], dst, sent, received, to_plane(plane))

    def share_from(plane):
        dst = share_in.at[plane]
        sent, received = share_sem.at[plane], share_in_sem.at[plane]
        return remote(share_out.at[plane], dst, sent, received, to_plane(plane))

    def part_to(line):
        dst = part_in.at[my_line]
        sent, received = part_sem.at[line], part_in_sem.at[my_line]
        return remote(part_out.at[line], dst, sent, received, to_line(line))

    def part_from(line):
        dst = part_in.at[line]
        sent, received = part_sem.at[line], part_in_sem.at[line]
        return remote(part_out.at[line], dst, sent, received, to_line(line))

    loads[4].wait()
    loads[5].wait()
    pl.semaphore_wait(barrier, lines + planes)
    page_to(1).start()
    page_to(2).start()
    tokens_to(my_line ^ 1).start()
    tokens_to(my_line ^ 3).start()

    pairs = pair_page_ref.shape[1]
    lanes = held.shape[2]
    for copy in loads[:4]:
        copy.wait()
    page_hot = (
        lax.broadcasted_iota(jnp.int32, (lanes, pairs), 0) == pair_page_ref[...]
    ).astype(jnp.float32)
    query_hot = lax.broadcasted_iota(jnp.int32, (local_queries, pairs), 0) == pair_query_ref[...]
    counted = query_hot.astype(jnp.float32)
    labelled = counted * pair_label_ref[...].astype(jnp.float32)
    stacked = jnp.concatenate([counted, labelled], axis=0)
    flags = lax.dot_general(
        stacked, page_hot, (((1,), (1,)), ((), ())), preferred_element_type=jnp.float32
    )
    held[my_line, pl.ds(rows, flag_rows), :] = flags.astype(jnp.bfloat16)
    for step in range(1, lines):
        flags_to(my_line ^ step).start()

    offset = -0.5 * tokens_each * (math.log(patches) / 4.0 + 2.0)

    row_query = lax.broadcasted_iota(jnp.int32, (rows, flag_rows), 0) // tokens_each
    flag_row = lax.broadcasted_iota(jnp.int32, (rows, flag_rows), 1)
    count_pick = (flag_row == row_query).astype(jnp.bfloat16)
    label_pick = (flag_row == row_query + local_queries).astype(jnp.bfloat16)
    lane = lax.broadcasted_iota(jnp.int32, (1, lanes), 1)
    scale = 4.0 * math.log2(math.e)

    def logits(line, plane):
        return lax.dot_general(
            held[line, pl.ds(0, rows), :],
            paged[plane].reshape(patches, width),
            (((1,), (1,)), ((), ())),
            preferred_element_type=jnp.float32,
        )

    def weights(dots, line, plane):
        page = my_line * planes + plane
        own_lane = (lane == page).astype(jnp.float32)
        own_shift = 2.0 * jnp.sum((hot_ref[...] == page).astype(jnp.float32), keepdims=True)
        flag = held[line, pl.ds(rows, flag_rows), :]
        counts = jnp.sum(
            jnp.dot(count_pick, flag, preferred_element_type=jnp.float32) * own_lane,
            axis=1,
            keepdims=True,
        )
        labels = jnp.sum(
            jnp.dot(label_pick, flag, preferred_element_type=jnp.float32) * own_lane,
            axis=1,
            keepdims=True,
        )
        peak = jnp.max(dots, axis=1, keepdims=True)
        expo = jnp.exp2((dots - peak) * scale)
        totals = jnp.sum(expo, axis=1, keepdims=True)
        log_total = 4.0 * peak + jnp.log(totals)
        score = jnp.sum(log_total.reshape(local_queries, tokens_each, 1), axis=1, keepdims=True)
        score = jnp.broadcast_to(score, (local_queries, tokens_each, 1)).reshape(rows, 1)
        logit = 0.5 * (score / 4.0) + offset - own_shift
        slope = 0.5 * (counts * jax.nn.sigmoid(logit) - labels)
        return (expo * (slope / totals)).astype(jnp.bfloat16)

    started_lines, started_pages = set(), set()

    def gradients(weight, line, plane, first_line, first_page):
        tokens = held[line, pl.ds(0, rows), :]
        by_query = jnp.dot(
            weight, paged[plane].reshape(patches, width), preferred_element_type=jnp.float32
        )
        by_page = lax.dot_general(
            tokens, weight, (((0,), (0,)), ((), ())), preferred_element_type=jnp.float32
        )
        query_acc[line] = by_query if first_line else query_acc[line] + by_query
        for side in range(page_acc.shape[1]):
            terms = by_page[:, side * part : (side + 1) * part]
            page_acc[plane, side] = terms if first_page else page_acc[plane, side] + terms

    def block(*places):
        spots = [(my_line ^ hop, turn(jump)) for hop, jump in places]
        dots = [logits(*spot) for spot in spots]
        for spot, dot, (hop, jump) in zip(spots, dots, places):
            fresh = hop not in started_lines, jump not in started_pages
            started_lines.add(hop)
            started_pages.add(jump)
            gradients(weights(dot, *spot), *spot, *fresh)

    def half_page(plane):
        swap(plane).wait_recv()
        return page_acc[plane, core] + swap_in[plane].astype(jnp.float32)

    def act(kind, *what):
        if kind == "block":
            block(*what)
            return
        offset_by = what[0]
        line, plane = my_line ^ offset_by, turn(offset_by)
        if kind == "tokens":
            tokens_from(line).wait_recv()
            flags_from(line).wait_recv()
        elif kind == "send_tokens":
            tokens_to(line).start()
        elif kind == "sent_tokens":
            tokens_to(line).wait_send()
        elif kind == "send_page":
            page_on().start()
        elif kind == "sent_page":
            page_to(plane).wait_send()
        elif kind == "page":
            if offset_by < 3:
                page_from(plane, 1 - core).wait_recv()
            page_from(plane, core).wait_recv()
            relay(offset_by).start()
        elif kind == "relayed":
            relayed(offset_by).wait_recv()
        elif kind == "line":
            part_out[line] = query_acc[line].astype(jnp.bfloat16)
            part_to(line).start()
        elif kind == "finish":
            swap_out[plane] = page_acc[plane, 1 - core].astype(jnp.bfloat16)
            swap(plane).start()
        elif kind == "share":
            share_out[plane] = half_page(plane).astype(jnp.bfloat16)
            share_to(plane).start()

    block((0, 0))
    for step in plan():
        act(*step)

    total = query_acc[my_line]
    for step in range(1, lines):
        part_from(my_line ^ step).wait_recv()
        total += part_in[my_line ^ step].astype(jnp.float32)
    query_grad_ref[...] = total.astype(jnp.bfloat16)

    total = half_page(my_plane)
    for step in range(1, planes):
        share_from(my_plane ^ step).wait_recv()
        total += share_in[my_plane ^ step].astype(jnp.float32)
    page_grad_ref[...] = total.T.astype(jnp.bfloat16)

    swap(my_plane).wait_send()
    for step in range(1, lines):
        flags_to(my_line ^ step).wait_send()
        part_to(my_line ^ step).wait_send()
    for step in range(1, planes):
        plane = my_plane ^ step
        swap(plane).wait_send()
        share_to(plane).wait_send()
    relay(1).wait_send()
    relay(3).wait_send()
    tokens_to(my_line ^ 1).wait_send()
    tokens_to(my_line ^ 2).wait_send()
    tokens_to(my_line ^ 3).wait_send()
    page_to(1).wait_send()
    page_to(2).wait_send()
    page_on().wait_send()


def store_kernel(query_ref, page_ref, query_out, page_out, sems):
    copies = [
        pltpu.make_async_copy(query_ref, query_out, sems.at[0]),
        pltpu.make_async_copy(page_ref, page_out, sems.at[1]),
    ]
    for copy in copies:
        copy.start()
    for copy in copies:
        copy.wait()


def dense_shards(queries, pages, pair_page, pair_query, pair_label, hot_pages):
    owners = lax.axis_size("owner")
    replicas = lax.axis_size("replica")
    local_queries, tokens_each, width = queries.shape
    patches = pages.shape[1]
    pairs = pair_query.shape[0]
    rows = local_queries * tokens_each
    flag_rows = 2 * local_queries
    part = patches // replicas
    planes = math.isqrt(owners)
    lines = owners // planes
    vmem = pl.BlockSpec(memory_space=pltpu.VMEM)
    hbm = pl.BlockSpec(memory_space=pltpu.HBM)
    query_grad, page_grad = pl.pallas_call(
        functools.partial(
            dense_kernel, lines, planes, (local_queries, tokens_each, width, patches)
        ),
        out_shape=(
            jax.ShapeDtypeStruct((rows, width), jnp.bfloat16),
            jax.ShapeDtypeStruct((part, width), jnp.bfloat16),
        ),
        in_specs=[hbm] * 6,
        out_specs=(vmem, vmem),
        scratch_shapes=[
            *[pltpu.VMEM((1, pairs), jnp.int32)] * 3,
            pltpu.VMEM((1, hot_pages.shape[0]), jnp.int32),
            pltpu.VMEM((lines, rows + flag_rows, width), jnp.bfloat16),
            pltpu.VMEM((planes, replicas, part, width), jnp.bfloat16),
            pltpu.VMEM((planes, replicas, width, part), jnp.float32),
            pltpu.VMEM((lines, rows, width), jnp.float32),
            *[pltpu.VMEM((planes, width, part), jnp.bfloat16)] * 4,
            *[pltpu.VMEM((lines, rows, width), jnp.bfloat16)] * 2,
            pltpu.SemaphoreType.DMA((6,)),
            *[pltpu.SemaphoreType.DMA((lines,))] * 4,
            pltpu.SemaphoreType.DMA((planes,)),
            pltpu.SemaphoreType.DMA((planes, replicas)),
            *[pltpu.SemaphoreType.DMA((planes,))] * 6,
            *[pltpu.SemaphoreType.DMA((lines,))] * 2,
        ],
        compiler_params=pltpu.CompilerParams(
            collective_id=0, has_side_effects=True, vmem_limit_bytes=24 << 20
        ),
    )(
        *[
            pltpu.with_memory_space_constraint(operand, pltpu.HBM)
            for operand in (
                queries.reshape(rows, width),
                pages[0].reshape(replicas, part, width),
                pair_page.reshape(1, pairs),
                pair_query.reshape(1, pairs),
                pair_label.reshape(1, pairs),
                hot_pages.reshape(1, hot_pages.shape[0]),
            )
        ]
    )
    query_grad, page_grad = pl.pallas_call(
        store_kernel,
        out_shape=(
            jax.ShapeDtypeStruct(query_grad.shape, query_grad.dtype),
            jax.ShapeDtypeStruct(page_grad.shape, page_grad.dtype),
        ),
        in_specs=[vmem, vmem],
        out_specs=(hbm, hbm),
        scratch_shapes=[pltpu.SemaphoreType.DMA((2,))],
        compiler_params=pltpu.CompilerParams(vmem_limit_bytes=1 << 20),
    )(query_grad, page_grad)
    return query_grad.reshape(queries.shape), page_grad[None]


SHARPNESS = 4.0
SLOPE_SCALE = 0.5
HOT_SHIFT = 2.0


def score_block(token_rows, label_rows, page_rows, offset, shift):
    count = token_rows.shape[0]
    tokens_each = token_rows.shape[1]
    flat_rows = token_rows.reshape(count * tokens_each, token_rows.shape[2])
    logits = SHARPNESS * lax.dot_general(
        flat_rows, page_rows, (((1,), (1,)), ((), ())), preferred_element_type=jnp.float32
    )
    peak = jnp.max(logits, axis=1, keepdims=True)
    expo = jnp.exp(logits - peak)
    totals = jnp.sum(expo, axis=1, keepdims=True)
    log_total = peak + jnp.log(totals)
    score = jnp.sum(log_total.reshape(count, tokens_each), axis=1) / SHARPNESS
    logit = SLOPE_SCALE * score + offset - shift
    slope = SLOPE_SCALE * (jax.nn.sigmoid(logit) - label_rows[:, 0]) * label_rows[:, 1]
    slope_rows = jnp.repeat(slope, tokens_each)[:, None]
    weight = (expo / totals * slope_rows).astype(jnp.bfloat16)
    grads = jnp.dot(weight, page_rows, preferred_element_type=jnp.float32).astype(jnp.bfloat16)
    page_part = lax.dot_general(
        weight, flat_rows, (((0,), (0,)), ((), ())), preferred_element_type=jnp.float32
    )
    return (grads.reshape(token_rows.shape), page_part)


def sparse_shards(queries, pages, pair_page, pair_query, pair_label, hot_pages):
    owners = lax.axis_size("owner")
    owner_place = lax.axis_index("owner")
    local_pairs = pair_page.shape[0]
    local_queries = queries.shape[0]
    tokens_each = queries.shape[1]
    width = queries.shape[2]
    patch_count = pages.shape[1]
    capacity = max(2, 4 * local_pairs // owners)
    slots = owners * capacity
    offset = -SLOPE_SCALE * tokens_each * (math.log(patch_count) / SHARPNESS + SHARPNESS / 2.0)
    targets = pair_page[:, 0]
    owned_hot = (hot_pages == owner_place).astype(jnp.float32)
    target_hot = (targets[:, None] == jnp.arange(owners, dtype=jnp.int32)[None, :]).astype(
        jnp.int32
    )
    earlier = jnp.cumsum(target_hot, axis=0) - target_hot
    rank_within = jnp.sum(earlier * target_hot, axis=1)
    slot_of = targets * capacity + rank_within
    select = (slot_of[None, :] == jnp.arange(slots, dtype=jnp.int32)[:, None]).astype(jnp.bfloat16)
    query_hot = (pair_query[:, None] == jnp.arange(local_queries, dtype=jnp.int32)[None, :]).astype(
        jnp.bfloat16
    )
    pair_tokens = jnp.dot(
        query_hot,
        queries.reshape(local_queries, tokens_each * width),
        preferred_element_type=jnp.float32,
    ).astype(jnp.bfloat16)
    send_tokens = jnp.dot(select, pair_tokens, preferred_element_type=jnp.float32).astype(
        jnp.bfloat16
    )
    pair_flags = jnp.stack(
        [pair_label.astype(jnp.float32), jnp.ones((local_pairs,), jnp.float32)], axis=1
    ).astype(jnp.bfloat16)
    send_flags = jnp.dot(select, pair_flags, preferred_element_type=jnp.float32).astype(
        jnp.bfloat16
    )
    got_tokens, got_flags = (
        lax.all_to_all(
            send_tokens.reshape(owners, capacity * tokens_each * width),
            "owner",
            split_axis=0,
            concat_axis=0,
            tiled=True,
        ),
        lax.all_to_all(
            send_flags.reshape(owners, capacity * 2),
            "owner",
            split_axis=0,
            concat_axis=0,
            tiled=True,
        ),
    )
    slot_tokens = got_tokens.reshape(slots, tokens_each, width)
    slot_flags = got_flags.reshape(slots, 2).astype(jnp.float32)
    page_rows = pages[0]
    own_shift = HOT_SHIFT * jnp.sum(owned_hot)
    block_rows = slots // max(1, slots // 64)
    filled = (slot_flags[:, 1] > 0.5).astype(jnp.int32)
    order = jnp.argsort(1 - filled, stable=True)
    inverse = jnp.argsort(order, stable=True)
    sorted_tokens = slot_tokens[order]
    sorted_flags = slot_flags[order]
    live_blocks = (jnp.sum(filled) + block_rows - 1) // block_rows

    def visit(block_id, carry):
        grad_store, page_acc = carry
        start = (block_id * block_rows).astype(jnp.int32)
        token_rows = lax.dynamic_slice_in_dim(sorted_tokens, start, block_rows, 0)
        label_rows = lax.dynamic_slice_in_dim(sorted_flags, start, block_rows, 0)
        grads, page_part = score_block(token_rows, label_rows, page_rows, offset, own_shift)
        grad_store = lax.dynamic_update_slice_in_dim(grad_store, grads, start, 0)
        return (grad_store, page_acc + page_part)

    sorted_grads, page_terms = lax.fori_loop(
        0,
        live_blocks,
        visit,
        (
            jnp.zeros((slots, tokens_each, width), jnp.bfloat16),
            jnp.zeros((patch_count, width), jnp.float32),
        ),
    )
    slot_grads = sorted_grads[inverse]
    returned = lax.all_to_all(
        slot_grads.reshape(owners, capacity * tokens_each * width),
        "owner",
        split_axis=0,
        concat_axis=0,
        tiled=True,
    )
    pair_grads = lax.dot_general(
        select,
        returned.reshape(slots, tokens_each * width),
        (((0,), (0,)), ((), ())),
        preferred_element_type=jnp.float32,
    )
    summed = lax.dot_general(
        query_hot.astype(jnp.float32),
        pair_grads,
        (((0,), (0,)), ((), ())),
        precision=lax.Precision.HIGHEST,
        preferred_element_type=jnp.float32,
    )
    query_grad = summed.reshape(local_queries, tokens_each, width).astype(jnp.bfloat16)
    page_share = lax.psum_scatter(
        page_terms.astype(jnp.bfloat16), "replica", scatter_dimension=0, tiled=True
    )
    return (query_grad, page_share[None])


def shards(queries, pages, pair_page, pair_query, pair_label, hot_pages):
    owners = lax.axis_size("owner")
    replicas = lax.axis_size("replica")
    local_pairs = pair_query.shape[0]
    local_queries = queries.shape[0]
    capacity = max(2, 4 * local_pairs // owners)
    dense = capacity >= local_queries and owners <= queries.shape[2] and replicas == 2
    dense = dense and owners == len(ORDER) ** 2
    plan = dense_shards if dense else sparse_shards
    return plan(queries, pages, pair_page, pair_query, pair_label, hot_pages)


def solution(mesh):
    placed = (
        P(("owner", "replica"), None, None),
        P("owner", None, None),
        P(("owner", "replica"), None),
        P(("owner", "replica")),
        P(("owner", "replica")),
        P(),
    )
    return jax.shard_map(
        shards,
        mesh=mesh,
        in_specs=placed,
        out_specs=(P(("owner", "replica"), None, None), P("owner", "replica", None)),
        check_vma=False,
    )
```

```python
import functools
import math

import jax
import jax.numpy as jnp
from jax import lax
from jax.experimental import pallas as pl
from jax.experimental.pallas import tpu as pltpu
from jax.sharding import PartitionSpec as P

MESH = pl.DeviceIdType.MESH


ORDER = range(4)

def plan():
    return (
        ("tokens", 1),
        ("block", (1, 0)),
        ("send_tokens", 2),
        ("page", 1),
        ("send_page", 3),
        ("block", (0, 1), (1, 1)),
        ("tokens", 3),
        ("relayed", 2),
        ("block", (3, 1), (3, 0), (0, 2), (1, 2), (3, 2)),
        ("page", 3),
        ("tokens", 2),
        ("block", (2, 1), (2, 2)),
        ("finish", 1),
        ("finish", 2),
        ("relayed", 3),
        ("block", (3, 3), (1, 3)),
        ("line", 3),
        ("line", 1),
        ("share", 1),
        ("share", 2),
        ("last", (2, 3), (0, 3)),
        ("block", (2, 0)),
        ("line", 2),
        ("share", 3),
        ("finish", 0),
    )


def dense_kernel(
    lines,
    planes,
    shapes,
    query_ref,
    page_ref,
    pair_page_hbm,
    pair_query_hbm,
    pair_label_hbm,
    hot_hbm,
    query_grad_ref,
    page_grad_ref,
    pair_page_ref,
    pair_query_ref,
    pair_label_ref,
    hot_ref,
    held,
    paged,
    page_acc,
    query_acc,
    swap_out,
    swap_in,
    share_out,
    share_in,
    part_out,
    part_in,
    load_sem,
    line_sem,
    line_in_sem,
    flag_sem,
    flag_in_sem,
    plane_sem,
    plane_in_sem,
    relay_sem,
    relay_in_sem,
    swap_sem,
    swap_in_sem,
    share_sem,
    share_in_sem,
    part_sem,
    part_in_sem,
):
    local_queries, tokens_each, width, patches = shapes
    rows = local_queries * tokens_each
    flag_rows = held.shape[1] - rows
    part = page_acc.shape[3]
    me = lax.axis_index("owner")
    core = lax.axis_index("replica")
    my_line, my_plane = me // planes, me % planes

    def load(src, dst, place):
        return pltpu.make_async_copy(src, dst, load_sem.at[place])

    loads = [
        load(pair_page_hbm, pair_page_ref, 0),
        load(pair_query_hbm, pair_query_ref, 1),
        load(pair_label_hbm, pair_label_ref, 2),
        load(hot_hbm, hot_ref, 3),
        load(query_ref, held.at[my_line, pl.ds(0, rows), :], 4),
        load(page_ref, paged.at[my_plane], 5),
    ]

    barrier = pltpu.get_barrier_semaphore()

    def greet(owner):
        pl.semaphore_signal(barrier, inc=1, device_id={"owner": owner}, device_id_type=MESH)

    for step in range(1, lines):
        greet((my_line ^ step) * planes + my_plane)
    for step in range(1, planes):
        greet(my_line * planes + (my_plane ^ step))
    pl.semaphore_signal(barrier, inc=1, device_id={"replica": 1 - core}, device_id_type=MESH)
    across = {"owner": my_line * planes + (my_plane ^ (1 + core)), "replica": 1 - core}
    pl.semaphore_signal(barrier, inc=1, device_id=across, device_id_type=MESH)
    for copy in loads:
        copy.start()

    def remote(src, dst, sent, received, device):
        return pltpu.make_async_remote_copy(
            src_ref=src,
            dst_ref=dst,
            send_sem=sent,
            recv_sem=received,
            device_id=device,
            device_id_type=MESH,
        )

    def to_line(line):
        return {"owner": line * planes + my_plane}

    def to_plane(plane):
        return {"owner": my_line * planes + plane}

    twin = {"replica": 1 - core}

    def tokens_to(line):
        slot = held.at[my_line, pl.ds(0, rows), :]
        return remote(slot, slot, line_sem.at[line], line_in_sem.at[my_line], to_line(line))

    def tokens_from(line):
        slot = held.at[line, pl.ds(0, rows), :]
        return remote(slot, slot, line_sem.at[line], line_in_sem.at[line], to_line(line))

    def flags_to(line):
        slot = held.at[my_line, pl.ds(rows, flag_rows), :]
        return remote(slot, slot, flag_sem.at[line], flag_in_sem.at[my_line], to_line(line))

    def flags_from(line):
        slot = held.at[line, pl.ds(rows, flag_rows), :]
        return remote(slot, slot, flag_sem.at[line], flag_in_sem.at[line], to_line(line))

    def turn(jump):
        return my_plane ^ (0, 1 + core, 2 - core, 3)[jump]

    def page_to(jump):
        slot = paged.at[my_plane, core]
        plane = my_plane ^ jump
        device = {"owner": my_line * planes + plane, "replica": jump - 1}
        return remote(slot, slot, plane_sem.at[plane], plane_in_sem.at[my_plane, core], device)

    def page_on():
        slot = paged.at[turn(1), core]
        sent, received = plane_sem.at[turn(3)], plane_in_sem.at[turn(1), core]
        return remote(slot, slot, sent, received, to_plane(turn(2)))

    def page_from(plane, side):
        slot = paged.at[plane, side]
        sent, received = plane_sem.at[plane], plane_in_sem.at[plane, side]
        return remote(slot, slot, sent, received, to_plane(plane))

    def relay(jump):
        plane = turn(jump)
        slot = paged.at[plane] if jump < 3 else paged.at[plane, core]
        return remote(slot, slot, relay_sem.at[plane], relay_in_sem.at[plane], twin)

    def relayed(jump):
        plane = turn(jump)
        slot = paged.at[plane] if jump < 3 else paged.at[plane, 1 - core]
        return remote(slot, slot, relay_sem.at[plane], relay_in_sem.at[plane], twin)

    def swap(plane):
        return remote(
            swap_out.at[plane], swap_in.at[plane], swap_sem.at[plane], swap_in_sem.at[plane], twin
        )

    def share_to(plane):
        dst = share_in.at[my_plane]
        sent, received = share_sem.at[plane], share_in_sem.at[my_plane]
        return remote(share_out.at[plane], dst, sent, received, to_plane(plane))

    def share_from(plane):
        dst = share_in.at[plane]
        sent, received = share_sem.at[plane], share_in_sem.at[plane]
        return remote(share_out.at[plane], dst, sent, received, to_plane(plane))

    def part_to(line):
        dst = part_in.at[my_line]
        sent, received = part_sem.at[line], part_in_sem.at[my_line]
        return remote(part_out.at[line], dst, sent, received, to_line(line))

    def part_from(line):
        dst = part_in.at[line]
        sent, received = part_sem.at[line], part_in_sem.at[line]
        return remote(part_out.at[line], dst, sent, received, to_line(line))

    loads[4].wait()
    loads[5].wait()
    pl.semaphore_wait(barrier, lines + planes)
    page_to(1).start()
    page_to(2).start()
    tokens_to(my_line ^ 1).start()
    tokens_to(my_line ^ 3).start()

    pairs = pair_page_ref.shape[1]
    lanes = held.shape[2]
    for copy in loads[:4]:
        copy.wait()
    page_hot = (
        lax.broadcasted_iota(jnp.int32, (lanes, pairs), 0) == pair_page_ref[...]
    ).astype(jnp.float32)
    query_hot = lax.broadcasted_iota(jnp.int32, (local_queries, pairs), 0) == pair_query_ref[...]
    counted = query_hot.astype(jnp.float32)
    labelled = counted * pair_label_ref[...].astype(jnp.float32)
    stacked = jnp.concatenate([counted, labelled], axis=0)
    flags = lax.dot_general(
        stacked, page_hot, (((1,), (1,)), ((), ())), preferred_element_type=jnp.float32
    )
    held[my_line, pl.ds(rows, flag_rows), :] = flags.astype(jnp.bfloat16)
    for step in range(1, lines):
        flags_to(my_line ^ step).start()

    offset = -0.5 * tokens_each * (math.log(patches) / 4.0 + 2.0)

    row_query = lax.broadcasted_iota(jnp.int32, (rows, flag_rows), 0) // tokens_each
    flag_row = lax.broadcasted_iota(jnp.int32, (rows, flag_rows), 1)
    count_pick = (flag_row == row_query).astype(jnp.bfloat16)
    label_pick = (flag_row == row_query + local_queries).astype(jnp.bfloat16)
    lane = lax.broadcasted_iota(jnp.int32, (1, lanes), 1)
    scale = 4.0 * math.log2(math.e)

    def logits(line, plane):
        return lax.dot_general(
            held[line, pl.ds(0, rows), :],
            paged[plane].reshape(patches, width),
            (((1,), (1,)), ((), ())),
            preferred_element_type=jnp.float32,
        )

    def weights(dots, line, plane):
        page = my_line * planes + plane
        own_lane = (lane == page).astype(jnp.float32)
        own_shift = 2.0 * jnp.sum((hot_ref[...] == page).astype(jnp.float32), keepdims=True)
        flag = held[line, pl.ds(rows, flag_rows), :]
        counts = jnp.sum(
            jnp.dot(count_pick, flag, preferred_element_type=jnp.float32) * own_lane,
            axis=1,
            keepdims=True,
        )
        labels = jnp.sum(
            jnp.dot(label_pick, flag, preferred_element_type=jnp.float32) * own_lane,
            axis=1,
            keepdims=True,
        )
        peak = jnp.max(dots, axis=1, keepdims=True)
        expo = jnp.exp2((dots - peak) * scale)
        totals = jnp.sum(expo, axis=1, keepdims=True)
        log_total = 4.0 * peak + jnp.log(totals)
        score = jnp.sum(log_total.reshape(local_queries, tokens_each, 1), axis=1, keepdims=True)
        score = jnp.broadcast_to(score, (local_queries, tokens_each, 1)).reshape(rows, 1)
        logit = 0.5 * (score / 4.0) + offset - own_shift
        slope = 0.5 * (counts * jax.nn.sigmoid(logit) - labels)
        return (expo * (slope / totals)).astype(jnp.bfloat16)

    started_lines, started_pages = set(), set()

    def gradients(weight, line, plane, first_line, first_page):
        tokens = held[line, pl.ds(0, rows), :]
        by_query = jnp.dot(
            weight, paged[plane].reshape(patches, width), preferred_element_type=jnp.float32
        )
        by_page = lax.dot_general(
            tokens, weight, (((0,), (0,)), ((), ())), preferred_element_type=jnp.float32
        )
        query_acc[line] = by_query if first_line else query_acc[line] + by_query
        for side in range(page_acc.shape[1]):
            terms = by_page[:, side * part : (side + 1) * part]
            page_acc[plane, side] = terms if first_page else page_acc[plane, side] + terms

    def last(*places):
        spots = [(my_line ^ hop, turn(jump)) for hop, jump in places]
        dots = [logits(*spot) for spot in spots]
        final = [weights(dot, *spot) for spot, dot in zip(spots, dots)]
        plane = spots[0][1]
        for (line, _), weight in zip(spots, final):
            by_page = lax.dot_general(
                held[line, pl.ds(0, rows), :],
                weight,
                (((0,), (0,)), ((), ())),
                preferred_element_type=jnp.float32,
            )
            for side in range(page_acc.shape[1]):
                terms = by_page[:, side * part : (side + 1) * part]
                page_acc[plane, side] = page_acc[plane, side] + terms
        act("finish", places[0][1])
        for (line, _), weight in zip(spots, final):
            query_acc[line] += jnp.dot(
                weight, paged[plane].reshape(patches, width), preferred_element_type=jnp.float32
            )

    def block(*places):
        spots = [(my_line ^ hop, turn(jump)) for hop, jump in places]
        dots = [logits(*spot) for spot in spots]
        for spot, dot, (hop, jump) in zip(spots, dots, places):
            fresh = hop not in started_lines, jump not in started_pages
            started_lines.add(hop)
            started_pages.add(jump)
            gradients(weights(dot, *spot), *spot, *fresh)

    def half_page(plane):
        swap(plane).wait_recv()
        return page_acc[plane, core] + swap_in[plane].astype(jnp.float32)

    def act(kind, *what):
        if kind == "block":
            block(*what)
            return
        if kind == "last":
            last(*what)
            return
        offset_by = what[0]
        line, plane = my_line ^ offset_by, turn(offset_by)
        if kind == "tokens":
            tokens_from(line).wait_recv()
            flags_from(line).wait_recv()
        elif kind == "send_tokens":
            tokens_to(line).start()
        elif kind == "sent_tokens":
            tokens_to(line).wait_send()
        elif kind == "send_page":
            page_on().start()
        elif kind == "sent_page":
            page_to(plane).wait_send()
        elif kind == "page":
            if offset_by < 3:
                page_from(plane, 1 - core).wait_recv()
            page_from(plane, core).wait_recv()
            relay(offset_by).start()
        elif kind == "relayed":
            relayed(offset_by).wait_recv()
        elif kind == "line":
            part_out[line] = query_acc[line].astype(jnp.bfloat16)
            part_to(line).start()
        elif kind == "finish":
            swap_out[plane] = page_acc[plane, 1 - core].astype(jnp.bfloat16)
            swap(plane).start()
        elif kind == "share":
            share_out[plane] = half_page(plane).astype(jnp.bfloat16)
            share_to(plane).start()

    block((0, 0))
    for step in plan():
        act(*step)

    total = query_acc[my_line]
    for step in range(1, lines):
        part_from(my_line ^ step).wait_recv()
        total += part_in[my_line ^ step].astype(jnp.float32)
    query_grad_ref[...] = total.astype(jnp.bfloat16)

    total = half_page(my_plane)
    for step in range(1, planes):
        share_from(my_plane ^ step).wait_recv()
        total += share_in[my_plane ^ step].astype(jnp.float32)
    page_grad_ref[...] = total.T.astype(jnp.bfloat16)

    swap(my_plane).wait_send()
    for step in range(1, lines):
        flags_to(my_line ^ step).wait_send()
        part_to(my_line ^ step).wait_send()
    for step in range(1, planes):
        plane = my_plane ^ step
        swap(plane).wait_send()
        share_to(plane).wait_send()
    relay(1).wait_send()
    relay(3).wait_send()
    tokens_to(my_line ^ 1).wait_send()
    tokens_to(my_line ^ 2).wait_send()
    tokens_to(my_line ^ 3).wait_send()
    page_to(1).wait_send()
    page_to(2).wait_send()
    page_on().wait_send()


def store_kernel(query_ref, page_ref, query_out, page_out, sems):
    copies = [
        pltpu.make_async_copy(query_ref, query_out, sems.at[0]),
        pltpu.make_async_copy(page_ref, page_out, sems.at[1]),
    ]
    for copy in copies:
        copy.start()
    for copy in copies:
        copy.wait()


def dense_shards(queries, pages, pair_page, pair_query, pair_label, hot_pages):
    owners = lax.axis_size("owner")
    replicas = lax.axis_size("replica")
    local_queries, tokens_each, width = queries.shape
    patches = pages.shape[1]
    pairs = pair_query.shape[0]
    rows = local_queries * tokens_each
    flag_rows = 2 * local_queries
    part = patches // replicas
    planes = math.isqrt(owners)
    lines = owners // planes
    vmem = pl.BlockSpec(memory_space=pltpu.VMEM)
    hbm = pl.BlockSpec(memory_space=pltpu.HBM)
    query_grad, page_grad = pl.pallas_call(
        functools.partial(
            dense_kernel, lines, planes, (local_queries, tokens_each, width, patches)
        ),
        out_shape=(
            jax.ShapeDtypeStruct((rows, width), jnp.bfloat16),
            jax.ShapeDtypeStruct((part, width), jnp.bfloat16),
        ),
        in_specs=[hbm] * 6,
        out_specs=(vmem, vmem),
        scratch_shapes=[
            *[pltpu.VMEM((1, pairs), jnp.int32)] * 3,
            pltpu.VMEM((1, hot_pages.shape[0]), jnp.int32),
            pltpu.VMEM((lines, rows + flag_rows, width), jnp.bfloat16),
            pltpu.VMEM((planes, replicas, part, width), jnp.bfloat16),
            pltpu.VMEM((planes, replicas, width, part), jnp.float32),
            pltpu.VMEM((lines, rows, width), jnp.float32),
            *[pltpu.VMEM((planes, width, part), jnp.bfloat16)] * 4,
            *[pltpu.VMEM((lines, rows, width), jnp.bfloat16)] * 2,
            pltpu.SemaphoreType.DMA((6,)),
            *[pltpu.SemaphoreType.DMA((lines,))] * 4,
            pltpu.SemaphoreType.DMA((planes,)),
            pltpu.SemaphoreType.DMA((planes, replicas)),
            *[pltpu.SemaphoreType.DMA((planes,))] * 6,
            *[pltpu.SemaphoreType.DMA((lines,))] * 2,
        ],
        compiler_params=pltpu.CompilerParams(
            collective_id=0, has_side_effects=True, vmem_limit_bytes=24 << 20
        ),
    )(
        *[
            pltpu.with_memory_space_constraint(operand, pltpu.HBM)
            for operand in (
                queries.reshape(rows, width),
                pages[0].reshape(replicas, part, width),
                pair_page.reshape(1, pairs),
                pair_query.reshape(1, pairs),
                pair_label.reshape(1, pairs),
                hot_pages.reshape(1, hot_pages.shape[0]),
            )
        ]
    )
    query_grad, page_grad = pl.pallas_call(
        store_kernel,
        out_shape=(
            jax.ShapeDtypeStruct(query_grad.shape, query_grad.dtype),
            jax.ShapeDtypeStruct(page_grad.shape, page_grad.dtype),
        ),
        in_specs=[vmem, vmem],
        out_specs=(hbm, hbm),
        scratch_shapes=[pltpu.SemaphoreType.DMA((2,))],
        compiler_params=pltpu.CompilerParams(vmem_limit_bytes=1 << 20),
    )(query_grad, page_grad)
    return query_grad.reshape(queries.shape), page_grad[None]


SHARPNESS = 4.0
SLOPE_SCALE = 0.5
HOT_SHIFT = 2.0


def score_block(token_rows, label_rows, page_rows, offset, shift):
    count = token_rows.shape[0]
    tokens_each = token_rows.shape[1]
    flat_rows = token_rows.reshape(count * tokens_each, token_rows.shape[2])
    logits = SHARPNESS * lax.dot_general(
        flat_rows, page_rows, (((1,), (1,)), ((), ())), preferred_element_type=jnp.float32
    )
    peak = jnp.max(logits, axis=1, keepdims=True)
    expo = jnp.exp(logits - peak)
    totals = jnp.sum(expo, axis=1, keepdims=True)
    log_total = peak + jnp.log(totals)
    score = jnp.sum(log_total.reshape(count, tokens_each), axis=1) / SHARPNESS
    logit = SLOPE_SCALE * score + offset - shift
    slope = SLOPE_SCALE * (jax.nn.sigmoid(logit) - label_rows[:, 0]) * label_rows[:, 1]
    slope_rows = jnp.repeat(slope, tokens_each)[:, None]
    weight = (expo / totals * slope_rows).astype(jnp.bfloat16)
    grads = jnp.dot(weight, page_rows, preferred_element_type=jnp.float32).astype(jnp.bfloat16)
    page_part = lax.dot_general(
        weight, flat_rows, (((0,), (0,)), ((), ())), preferred_element_type=jnp.float32
    )
    return (grads.reshape(token_rows.shape), page_part)


def sparse_shards(queries, pages, pair_page, pair_query, pair_label, hot_pages):
    owners = lax.axis_size("owner")
    owner_place = lax.axis_index("owner")
    local_pairs = pair_page.shape[0]
    local_queries = queries.shape[0]
    tokens_each = queries.shape[1]
    width = queries.shape[2]
    patch_count = pages.shape[1]
    capacity = max(2, 4 * local_pairs // owners)
    slots = owners * capacity
    offset = -SLOPE_SCALE * tokens_each * (math.log(patch_count) / SHARPNESS + SHARPNESS / 2.0)
    targets = pair_page[:, 0]
    owned_hot = (hot_pages == owner_place).astype(jnp.float32)
    target_hot = (targets[:, None] == jnp.arange(owners, dtype=jnp.int32)[None, :]).astype(
        jnp.int32
    )
    earlier = jnp.cumsum(target_hot, axis=0) - target_hot
    rank_within = jnp.sum(earlier * target_hot, axis=1)
    slot_of = targets * capacity + rank_within
    select = (slot_of[None, :] == jnp.arange(slots, dtype=jnp.int32)[:, None]).astype(jnp.bfloat16)
    query_hot = (pair_query[:, None] == jnp.arange(local_queries, dtype=jnp.int32)[None, :]).astype(
        jnp.bfloat16
    )
    pair_tokens = jnp.dot(
        query_hot,
        queries.reshape(local_queries, tokens_each * width),
        preferred_element_type=jnp.float32,
    ).astype(jnp.bfloat16)
    send_tokens = jnp.dot(select, pair_tokens, preferred_element_type=jnp.float32).astype(
        jnp.bfloat16
    )
    pair_flags = jnp.stack(
        [pair_label.astype(jnp.float32), jnp.ones((local_pairs,), jnp.float32)], axis=1
    ).astype(jnp.bfloat16)
    send_flags = jnp.dot(select, pair_flags, preferred_element_type=jnp.float32).astype(
        jnp.bfloat16
    )
    got_tokens, got_flags = (
        lax.all_to_all(
            send_tokens.reshape(owners, capacity * tokens_each * width),
            "owner",
            split_axis=0,
            concat_axis=0,
            tiled=True,
        ),
        lax.all_to_all(
            send_flags.reshape(owners, capacity * 2),
            "owner",
            split_axis=0,
            concat_axis=0,
            tiled=True,
        ),
    )
    slot_tokens = got_tokens.reshape(slots, tokens_each, width)
    slot_flags = got_flags.reshape(slots, 2).astype(jnp.float32)
    page_rows = pages[0]
    own_shift = HOT_SHIFT * jnp.sum(owned_hot)
    block_rows = slots // max(1, slots // 64)
    filled = (slot_flags[:, 1] > 0.5).astype(jnp.int32)
    order = jnp.argsort(1 - filled, stable=True)
    inverse = jnp.argsort(order, stable=True)
    sorted_tokens = slot_tokens[order]
    sorted_flags = slot_flags[order]
    live_blocks = (jnp.sum(filled) + block_rows - 1) // block_rows

    def visit(block_id, carry):
        grad_store, page_acc = carry
        start = (block_id * block_rows).astype(jnp.int32)
        token_rows = lax.dynamic_slice_in_dim(sorted_tokens, start, block_rows, 0)
        label_rows = lax.dynamic_slice_in_dim(sorted_flags, start, block_rows, 0)
        grads, page_part = score_block(token_rows, label_rows, page_rows, offset, own_shift)
        grad_store = lax.dynamic_update_slice_in_dim(grad_store, grads, start, 0)
        return (grad_store, page_acc + page_part)

    sorted_grads, page_terms = lax.fori_loop(
        0,
        live_blocks,
        visit,
        (
            jnp.zeros((slots, tokens_each, width), jnp.bfloat16),
            jnp.zeros((patch_count, width), jnp.float32),
        ),
    )
    slot_grads = sorted_grads[inverse]
    returned = lax.all_to_all(
        slot_grads.reshape(owners, capacity * tokens_each * width),
        "owner",
        split_axis=0,
        concat_axis=0,
        tiled=True,
    )
    pair_grads = lax.dot_general(
        select,
        returned.reshape(slots, tokens_each * width),
        (((0,), (0,)), ((), ())),
        preferred_element_type=jnp.float32,
    )
    summed = lax.dot_general(
        query_hot.astype(jnp.float32),
        pair_grads,
        (((0,), (0,)), ((), ())),
        precision=lax.Precision.HIGHEST,
        preferred_element_type=jnp.float32,
    )
    query_grad = summed.reshape(local_queries, tokens_each, width).astype(jnp.bfloat16)
    page_share = lax.psum_scatter(
        page_terms.astype(jnp.bfloat16), "replica", scatter_dimension=0, tiled=True
    )
    return (query_grad, page_share[None])


def shards(queries, pages, pair_page, pair_query, pair_label, hot_pages):
    owners = lax.axis_size("owner")
    replicas = lax.axis_size("replica")
    local_pairs = pair_query.shape[0]
    local_queries = queries.shape[0]
    capacity = max(2, 4 * local_pairs // owners)
    dense = capacity >= local_queries and owners <= queries.shape[2] and replicas == 2
    dense = dense and owners == len(ORDER) ** 2
    plan = dense_shards if dense else sparse_shards
    return plan(queries, pages, pair_page, pair_query, pair_label, hot_pages)


def solution(mesh):
    placed = (
        P(("owner", "replica"), None, None),
        P("owner", None, None),
        P(("owner", "replica"), None),
        P(("owner", "replica")),
        P(("owner", "replica")),
        P(),
    )
    return jax.shard_map(
        shards,
        mesh=mesh,
        in_specs=placed,
        out_specs=(P(("owner", "replica"), None, None), P("owner", "replica", None)),
        check_vma=False,
    )
```
